128 devices in a mesh: gy: 8 (over z, y_hi), gz: 16 (over y_lo, x, core).
Axes of the slice: x: 4, y: 4 (y_hi: 2, y_lo: 2; y = y_hi * 2 + y_lo), z: 4, core: 2. Of those that a mesh axis runs over, the one named last changes fastest.
Arguments:
- fields: bfloat16 [1024, 32, 128, 64], P(None, 'gy', 'gz'), may hold values from -6 to 6
- spec_weight: float32 [32, 2, 64, 64], P('gz'), may hold values from -1.5 to 1.5
- skip_weight: bfloat16 [64, 64], replicated, may hold values from -0.75 to 0.75
- up_weight: bfloat16 [64, 256], replicated, may hold values from -0.75 to 0.75
- down_weight: bfloat16 [256, 64], replicated, may hold values from -0.375 to 0.375
- cotangent: bfloat16 [1024, 32, 128, 64], P(None, 'gy', 'gz'), may hold values from -6 to 6
Outputs:
- output: bfloat16 [1024, 32, 128, 64], P(None, 'gy', 'gz')
- grad_fields: bfloat16 [1024, 32, 128, 64], P(None, 'gy', 'gz')
- grad_spec: float32 [32, 2, 64, 64], P('gz')
- grad_skip: float32 [64, 64], replicated
- grad_up: float32 [64, 256], replicated
- grad_down: float32 [256, 64], replicated
The draws below stay inside these ranges and needn't reach their ends.
All inputs are finite; a program needn't handle non-finite values.
Results may differ from the reference program's by a relative error of at most 0.0067.
Values sent between devices are 32-bit elements; how exact they have to be, the bound alone decides.
No kernel may reach another device: no remote copies, remote signals or barrier semaphores. Data moves between devices by JAX's collectives and lax.ppermute only.
A program may use at most 192 MiB of HBM per device.

```python
import math
import jax
import jax.numpy as jnp
from jax import lax

NX = 1024
CH = 64
MODES = 32
HID = 256
NY = 32
NZ = 128


def levels(stream_key, shape, split, low, largest):
    def one(dim, parts):
        steps = jax.random.uniform(jax.random.fold_in(jax.random.fold_in(stream_key, 6), dim), (parts,), jnp.float32, low / len(split), largest / len(split))
        return jnp.repeat(jnp.exp(steps), shape[dim] // parts).reshape((-1,) + (1,) * (len(shape) - dim - 1))

    loudness = one(*split[0])
    for cut in split[1:]:
        loudness = loudness * one(*cut)
    return loudness


def gaussian(own_key, dims, width, most, shards=(), kind=jnp.bfloat16):
    values = jax.random.normal(own_key, dims, jnp.float32) * width
    if len(shards) > 0:
        values = levels(own_key, dims, shards, -0.22, 0.18) * values
    return jnp.clip(values, min=-most, max=most).astype(kind)


def setup_inputs(seed: int = 0) -> dict:
    key_list = jax.random.split(jax.random.key(seed), 7)
    return {
        "fields": gaussian(key_list[0], (NX, NY, NZ, CH), 1.0, 6.0, ((1, 8), (2, 16))),
        "spec_weight": gaussian(key_list[1], (MODES, 2, CH, CH), 0.25, 1.5, ((0, 16),), jnp.float32),
        "skip_weight": gaussian(key_list[2], (CH, CH), CH ** -0.5, 0.75),
        "up_weight": gaussian(key_list[3], (CH, HID), CH ** -0.5, 0.75),
        "down_weight": gaussian(key_list[4], (HID, CH), HID ** -0.5, 0.375),
        "cotangent": gaussian(key_list[5], (NX, NY, NZ, CH), 1.0, 6.0, ((1, 8), (2, 16))),
    }


def fourier_tables(length_x, kept):
    position = jnp.arange(length_x, dtype=jnp.int32)[:, None]
    wavenum = jnp.arange(kept, dtype=jnp.int32)[None, :]
    phase = (position * wavenum % length_x).astype(jnp.float32) * (2.0 * math.pi / length_x)
    factor = 1.0 / math.sqrt(length_x)
    analysis = jnp.concatenate([jnp.cos(phase), -jnp.sin(phase)], axis=1) * factor
    doubled = jnp.where(wavenum == 0, 1.0, 2.0).astype(jnp.float32)
    synthesis = jnp.concatenate([jnp.cos(phase) * doubled, -jnp.sin(phase) * doubled], axis=1) * factor
    return (analysis, synthesis)

def to_spectra(stacked, pencils, channels):
    kept = stacked.shape[0] // 2
    return stacked.reshape(2, kept, pencils, channels).transpose(1, 2, 0, 3).reshape(kept, pencils, 2 * channels)

def from_spectra(spectra, channels):
    kept = spectra.shape[0]
    pencils = spectra.shape[1]
    return spectra.reshape(kept, pencils, 2, channels).transpose(2, 0, 1, 3).reshape(2 * kept, pencils * channels)

def mixer_of(weight):
    real_part = weight[:, 0]
    imag_part = weight[:, 1]
    upper = jnp.concatenate([real_part, imag_part], axis=2)
    lower = jnp.concatenate([-imag_part, real_part], axis=2)
    return jnp.concatenate([upper, lower], axis=1)

def weight_grad(moment, channels):
    real_grad = moment[:, :channels, :channels] + moment[:, channels:, channels:]
    imag_grad = moment[:, :channels, channels:] - moment[:, channels:, :channels]
    return jnp.stack([real_grad, imag_grad], axis=1)

def contract_rows(left, right):
    return lax.dot_general(left, right, (((0,), (0,)), ((), ())), preferred_element_type=jnp.float32)

def local_pass(rows_u, rows_s, rows_g, skip_weight, up_weight, down_weight):
    pre_act = rows_s + jnp.dot(rows_u, skip_weight, preferred_element_type=jnp.float32)
    act_full, act_pull = jax.vjp(jax.nn.gelu, pre_act)
    act = act_full.astype(jnp.bfloat16)
    hidden_pre = jnp.dot(act, up_weight, preferred_element_type=jnp.float32)
    hidden_full, hidden_pull = jax.vjp(jax.nn.gelu, hidden_pre)
    hidden = hidden_full.astype(jnp.bfloat16)
    result = jnp.dot(hidden, down_weight, preferred_element_type=jnp.float32).astype(jnp.bfloat16)
    grad_down = contract_rows(hidden, rows_g)
    hidden_cot = jnp.dot(rows_g, down_weight.T, preferred_element_type=jnp.float32)
    hidden_grad = hidden_pull(hidden_cot)[0].astype(jnp.bfloat16)
    grad_up = contract_rows(act, hidden_grad)
    act_cot = jnp.dot(hidden_grad, up_weight.T, preferred_element_type=jnp.float32)
    pre_grad = act_pull(act_cot)[0].astype(jnp.bfloat16)
    grad_skip = contract_rows(rows_u, pre_grad)
    local_cot = jnp.dot(pre_grad, skip_weight.T, preferred_element_type=jnp.float32)
    return (result, pre_grad, local_cot, grad_skip, grad_up, grad_down)

def reference(fields, spec_weight, skip_weight, up_weight, down_weight, cotangent):
    highest = lax.Precision.HIGHEST
    analysis, synthesis = fourier_tables(NX, MODES)
    analysis_low = analysis.astype(jnp.bfloat16)
    synthesis_low = synthesis.astype(jnp.bfloat16)
    by_row = jnp.moveaxis(fields, 1, 0)
    cot_row = jnp.moveaxis(cotangent, 1, 0)

    def forward_row(block):
        flat = block.reshape(NX, NZ * CH)
        return to_spectra(jnp.dot(analysis_low.T, flat, preferred_element_type=jnp.float32), NZ, CH)
    spectra = lax.map(forward_row, by_row)
    mixer = mixer_of(spec_weight)
    mixed = jnp.einsum('ykpi,kio->ykpo', spectra, mixer, precision=highest)

    def middle_row(operands):
        block, mixed_row, cot_block = operands
        field_sum = jnp.dot(synthesis, from_spectra(mixed_row, CH), precision=highest)
        result, pre_grad, local_cot, part_skip, part_up, part_down = local_pass(block.reshape(NX * NZ, CH), field_sum.reshape(NX * NZ, CH), cot_block.reshape(NX * NZ, CH), skip_weight, up_weight, down_weight)
        coeff_grad = to_spectra(jnp.dot(synthesis_low.T, pre_grad.reshape(NX, NZ * CH), preferred_element_type=jnp.float32), NZ, CH)
        return (result.reshape(NX, NZ, CH), local_cot.reshape(NX, NZ * CH), coeff_grad, part_skip, part_up, part_down)
    outputs, local_cots, coeff_grads, skip_parts, up_parts, down_parts = lax.map(middle_row, (by_row, mixed, cot_row))
    moment = jnp.einsum('ykpi,ykpo->kio', spectra, coeff_grads, precision=highest)
    back_spectra = jnp.einsum('ykpo,kio->ykpi', coeff_grads, mixer, precision=highest)

    def final_row(operands):
        local_cot, back_row = operands
        total = local_cot + jnp.dot(analysis, from_spectra(back_row, CH), precision=highest)
        return total.astype(jnp.bfloat16).reshape(NX, NZ, CH)
    grad_rows = lax.map(final_row, (local_cots, back_spectra))
    cell_scale = 1.0 / math.sqrt(NX * NY * NZ)
    pencil_scale = 1.0 / math.sqrt(NY * NZ)
    return (jnp.moveaxis(outputs, 0, 1), jnp.moveaxis(grad_rows, 0, 1), weight_grad(moment, CH) * pencil_scale, lax.optimization_barrier(jnp.sum(skip_parts, axis=0)) * cell_scale, lax.optimization_barrier(jnp.sum(up_parts, axis=0)) * cell_scale, lax.optimization_barrier(jnp.sum(down_parts, axis=0)) * cell_scale)
```

```python
import functools
import math

import jax
import jax.numpy as jnp
from jax import lax
from jax.experimental import pallas as pl
from jax.experimental.pallas import tpu as pltpu
from jax.sharding import PartitionSpec as P

MODES = 32
BF16 = jnp.bfloat16
F32 = jnp.float32
CHUNK = 256


def sent_to_all(shard, axis):
    peers = lax.axis_size(axis)
    return lax.all_to_all(
        jnp.broadcast_to(shard[None], (peers, *shard.shape)), axis, 0, 0, tiled=True
    )


def fourier_tables(length_x, kept):
    position = jnp.arange(length_x, dtype=jnp.int32)[:, None]
    wavenum = jnp.arange(kept, dtype=jnp.int32)[None, :]
    phase = (position * wavenum % length_x).astype(F32) * (2.0 * math.pi / length_x)
    factor = 1.0 / math.sqrt(length_x)
    analysis = jnp.concatenate([jnp.cos(phase), -jnp.sin(phase)], axis=1) * factor
    doubled = jnp.where(wavenum == 0, 1.0, 2.0).astype(F32)
    synthesis = (
        jnp.concatenate([jnp.cos(phase) * doubled, -jnp.sin(phase) * doubled], axis=1) * factor
    )
    return (analysis, synthesis)


def mm(a, b):
    return jnp.dot(a, b, preferred_element_type=F32)


def mm_nt(a, b):
    return lax.dot_general(a, b, (((1,), (1,)), ((), ())), preferred_element_type=F32)


def mm_tn(a, b):
    return lax.dot_general(a, b, (((0,), (0,)), ((), ())), preferred_element_type=F32)


def gelu_pair(x):
    c = math.sqrt(2.0 / math.pi)
    a = 0.044715
    x2 = x * x
    s = 0.5 * jnp.tanh(x * (x2 * (c * a) + c)) + 0.5
    g = x * s
    slope = s + (g - g * s) * (x2 * (6.0 * c * a) + 2.0 * c)
    return g, slope


def spectra_kernel(u_ref, ana_ref, t_ref):
    for i in range(u_ref.shape[0]):
        t_ref[i] = mm(u_ref[i], ana_ref[...]).T


def split_lanes(even, odd):
    half = even.shape[-1] // 2
    first = lax.broadcasted_iota(jnp.int32, even.shape, 1) < half
    low = jnp.where(first, even, pltpu.roll(odd, half, 1))
    high = jnp.where(first, pltpu.roll(even, half, 1), odd)
    return low, high


def mode_rows(ref, k, pairs):
    stride = 2 * MODES
    re = ref[pl.ds(k, pairs, stride=stride), :]
    im = ref[pl.ds(MODES + k, pairs, stride=stride), :]
    return jnp.concatenate(split_lanes(re, im), axis=0)


def put_mode_rows(ref, k, pairs, rows):
    stride = 2 * MODES
    re, im = split_lanes(rows[:pairs], rows[pairs:])
    ref[pl.ds(k, pairs, stride=stride), :] = re
    ref[pl.ds(MODES + k, pairs, stride=stride), :] = im


def mixer_of(upper):
    half = upper.shape[-1] // 2
    sign = jnp.where(lax.broadcasted_iota(jnp.int32, upper.shape, 1) < half, -1.0, 1.0)
    return jnp.concatenate([upper, pltpu.roll(upper, half, 1) * sign], axis=0).astype(BF16)


def main_kernel(
    t_ref, w_ref, u_ref, g_ref, skip_t_ref, up_t_ref, up_ref, down_t_ref, down_ref, syn_ref,
    res_ref, pg_ref, pay_ref, b_ref,
    m_ref, c_ref, gu_ref, gd_ref, gs_ref,
):
    q = pl.program_id(0)
    pairs = pl.num_programs(0)
    n_pairs = t_ref.shape[0] // (2 * MODES)
    length_x = u_ref.shape[-1]
    ch = up_ref.shape[0]

    @pl.when(q == 0)
    def _():
        gu_ref[...] = jnp.zeros_like(gu_ref)
        gd_ref[...] = jnp.zeros_like(gd_ref)
        gs_ref[...] = jnp.zeros_like(gs_ref)

        @pl.loop(0, MODES)
        def _(k):
            rows = mode_rows(t_ref, k, n_pairs).astype(BF16)
            put_mode_rows(m_ref, k, n_pairs, mm(rows, mixer_of(w_ref[k])))

    base = pl.multiple_of(q * (2 * MODES), 2 * MODES)
    mixed_t = m_ref[pl.ds(base, 2 * MODES), :].T.astype(BF16)
    lhs_pre = jnp.concatenate([skip_t_ref[...], mixed_t], axis=1)
    up_t, up, down_t, down = up_t_ref[...], up_ref[...], down_t_ref[...], down_ref[...]

    acc = jnp.zeros((2 * ch + 2 * MODES, 2 * ch), F32)
    gu = gu_ref[...]
    gd = gd_ref[...]
    for j in range(length_x // CHUNK):
        at = slice(j * CHUNK, (j + 1) * CHUNK)
        u = u_ref[0, :, at]
        g = g_ref[0, :, at]
        ut = jnp.concatenate([u, syn_ref[:, at]], axis=0)
        act, slope = gelu_pair(mm(lhs_pre, ut))
        act = act.astype(BF16)
        outs, grads = [], []
        for b in range(2):
            rows = slice(b * ch, (b + 1) * ch)
            hidden, hslope = gelu_pair(mm(up_t, act[rows]))
            hidden = hidden.astype(BF16)
            hgrad = (mm(down, g[rows]) * hslope).astype(BF16)
            outs.append(mm(down_t, hidden))
            gd += mm_nt(g[rows], hidden)
            grads.append(mm(up, hgrad))
            gu += mm_nt(act[rows], hgrad)
        res_ref[0, :, at] = jnp.concatenate(outs, axis=0).astype(BF16)
        pg = (jnp.concatenate(grads, axis=0) * slope).astype(BF16)
        pg_ref[0, :, at] = pg
        acc += mm_nt(ut, pg)
    gu_ref[...] = gu
    gd_ref[...] = gd
    gs_ref[...] += acc[: 2 * ch]
    c_ref[pl.ds(base, 2 * MODES), :] = acc[2 * ch :]

    @pl.when(q == pairs - 1)
    def _():
        owners = pay_ref.shape[0]
        kept = MODES // owners
        half = jnp.where(lax.broadcasted_iota(jnp.int32, (ch, 2 * ch), 1) < ch, 1.0, -1.0)

        @pl.loop(0, MODES)
        def _(k):
            spec = mode_rows(t_ref, k, n_pairs).astype(BF16)
            coef = mode_rows(c_ref, k, n_pairs).astype(BF16)
            put_mode_rows(b_ref, k, n_pairs, mm_nt(coef, mixer_of(w_ref[k])))
            moment = mm_tn(spec, coef)
            grad = moment[:ch] + pltpu.roll(moment[ch:], ch, 1) * half
            pay_ref[k // kept, pl.ds(pl.multiple_of((k % kept) * ch, ch), ch), :] = grad

        at = kept * ch
        part = ch // (owners // 2)
        skip = gs_ref[:ch] + pltpu.roll(gs_ref[ch:], ch, 1)
        small = ch // owners
        for o in range(owners):
            side, row = divmod(o, owners // 2)
            lanes = slice(side * 2 * ch, (side + 1) * 2 * ch)
            rows = slice(row * part, (row + 1) * part)
            pay_ref[o, at : at + part, :] = gu_ref[rows, lanes]
            pay_ref[o, at + part : at + 2 * part, :] = gd_ref[rows, lanes]
            pay_ref[o, at + 2 * part : at + 2 * part + small, :] = skip[o * small : (o + 1) * small]
            pay_ref[o, at + 2 * part + small :, :] = jnp.zeros((8 - small, 2 * ch), F32)


def final_kernel(pg_ref, b_ref, skip_ref, ana_ref, out_ref):
    back_t = b_ref[...].T.astype(BF16)
    lhs = jnp.concatenate([skip_ref[...], back_t], axis=1)
    rhs = jnp.concatenate([pg_ref[0], ana_ref[...]], axis=0)
    out_ref[0] = mm(lhs, rhs).astype(BF16)


def twice(weight):
    zeros = jnp.zeros_like(weight)
    upper = jnp.concatenate([weight, zeros], axis=1)
    lower = jnp.concatenate([zeros, weight], axis=1)
    return jnp.concatenate([upper, lower], axis=0)


def whole(shape):
    return pl.BlockSpec(shape, lambda *_: (0,) * len(shape))


def local(fields, spec_weight, skip_weight, up_weight, down_weight, cotangent):
    length_x, count_y, count_z, ch = fields.shape
    hid = up_weight.shape[1]
    pencils = count_y * count_z
    pairs = pencils // 2
    owners = lax.axis_size("gz")
    kept = MODES // owners
    analysis, synthesis = fourier_tables(length_x, MODES)
    analysis = analysis.astype(BF16)
    ana_t = analysis.T
    syn_t = synthesis.astype(BF16).T
    u = fields.transpose(1, 2, 3, 0).reshape(pairs, 2 * ch, length_x)
    g = cotangent.transpose(1, 2, 3, 0).reshape(pairs, 2 * ch, length_x)

    upper = jnp.concatenate([spec_weight[:, 0], spec_weight[:, 1]], axis=2)
    upper = upper.reshape(kept * ch, 2 * ch)
    gathered = sent_to_all(upper, "gz").reshape(MODES, ch, 2 * ch)

    step = 4
    big = lambda n: pl.BlockSpec((n, 2 * ch, length_x), lambda i: (i, 0, 0))
    spectra = pl.pallas_call(
        spectra_kernel,
        grid=(pairs // step,),
        in_specs=[big(step), whole((length_x, 2 * MODES))],
        out_specs=pl.BlockSpec((step, 2 * MODES, 2 * ch), lambda i: (i, 0, 0)),
        out_shape=jax.ShapeDtypeStruct((pairs, 2 * MODES, 2 * ch), F32),
        name="spectra",
    )(u, analysis).reshape(pairs * 2 * MODES, 2 * ch)

    rows = pairs * 2 * MODES
    wide = kept * ch + 2 * (2 * ch // owners) + 8
    result, pre_grad, payload, back = pl.pallas_call(
        main_kernel,
        grid=(pairs,),
        in_specs=[
            whole((rows, 2 * ch)),
            whole((MODES, ch, 2 * ch)),
            big(1),
            big(1),
            whole((2 * ch, 2 * ch)),
            whole((hid, ch)),
            whole((ch, hid)),
            whole((ch, hid)),
            whole((hid, ch)),
            whole((2 * MODES, length_x)),
        ],
        out_specs=[big(1), big(1), whole((owners, wide, 2 * ch)), whole((rows, 2 * ch))],
        out_shape=[
            jax.ShapeDtypeStruct((pairs, 2 * ch, length_x), BF16),
            jax.ShapeDtypeStruct((pairs, 2 * ch, length_x), BF16),
            jax.ShapeDtypeStruct((owners, wide, 2 * ch), F32),
            jax.ShapeDtypeStruct((rows, 2 * ch), F32),
        ],
        scratch_shapes=[
            pltpu.VMEM((rows, 2 * ch), F32),
            pltpu.VMEM((rows, 2 * ch), F32),
            pltpu.VMEM((ch, hid), F32),
            pltpu.VMEM((ch, hid), F32),
            pltpu.VMEM((2 * ch, 2 * ch), F32),
        ],
        name="main",
    )(
        spectra, gathered, u, g, twice(skip_weight.T), up_weight.T, up_weight, down_weight.T,
        down_weight, syn_t,
    )

    summed = lax.all_to_all(payload, "gz", 0, 0, tiled=True)
    grad_fields = pl.pallas_call(
        final_kernel,
        grid=(pairs,),
        in_specs=[
            big(1),
            pl.BlockSpec((2 * MODES, 2 * ch), lambda i: (i, 0)),
            whole((2 * ch, 2 * ch)),
            whole((2 * MODES, length_x)),
        ],
        out_specs=big(1),
        out_shape=jax.ShapeDtypeStruct((pairs, 2 * ch, length_x), BF16),
        name="final",
    )(pre_grad, back, twice(skip_weight), ana_t)

    total = sent_to_all(jnp.sum(summed, axis=0), "gy").sum(axis=0)
    all_pencils = pencils * lax.axis_size("gy") * owners
    cell_scale = 1.0 / math.sqrt(length_x * all_pencils)
    pencil_scale = 1.0 / math.sqrt(all_pencils)
    at = kept * ch
    part = 2 * ch // owners
    mine = total[:at].reshape(kept, ch, 2, ch).transpose(0, 2, 1, 3) * pencil_scale
    small = sent_to_all(total[at:] * cell_scale, "gz")

    def joined(block):
        return block.reshape(2, ch, 2 * ch).transpose(1, 0, 2).reshape(ch, hid)

    grad_up = joined(small[:, :part])
    grad_down = joined(small[:, part : 2 * part]).T
    grad_skip = small[:, 2 * part : 2 * part + ch // owners, :ch].reshape(ch, ch)

    def unpacked(x):
        return x.reshape(count_y, count_z, ch, length_x).transpose(3, 0, 1, 2)

    return (unpacked(result), unpacked(grad_fields), mine, grad_skip, grad_up, grad_down)


def solution(mesh):
    big = P(None, "gy", "gz", None)
    modes = P("gz", None, None, None)
    return jax.shard_map(
        local,
        mesh=mesh,
        in_specs=(big, modes, P(), P(), P(), big),
        out_specs=(big, big, modes, P(), P(), P()),
        check_vma=False,
    )
```

```python
import math

import jax
import jax.numpy as jnp
import numpy as np
from jax import lax
from jax.experimental import pallas as pl
from jax.experimental.pallas import tpu as pltpu
from jax.sharding import PartitionSpec as P

MODES = 32
BF16 = jnp.bfloat16
F32 = jnp.float32
CHUNK = 256
PER_STEP = 2
FINAL_STEP = 4
PRE_STEP = 2
SKEW = 2
UNROLL = 2


def to_group(block, axis, groups):
    peers = len(groups[0])
    return lax.all_to_all(
        jnp.broadcast_to(block[None], (peers, *block.shape)),
        axis, 0, 0, axis_index_groups=groups, tiled=True,
    )


def swapped(block, axis, mask):
    return lax.ppermute(block, axis, [(i, i ^ mask) for i in range(lax.axis_size(axis))])


def fourier_tables(length_x, kept):
    phase = np.outer(np.arange(length_x), np.arange(kept)) % length_x * (2.0 * np.pi / length_x)
    table = np.concatenate([np.cos(phase), -np.sin(phase)], axis=1) / math.sqrt(length_x)
    doubled = np.where(np.arange(2 * kept) % kept == 0, 1.0, 2.0)
    return table.astype(BF16), (table * doubled).astype(BF16)


def mm(a, b):
    return jnp.dot(a, b, preferred_element_type=F32)


def mm_nt(a, b):
    return lax.dot_general(a, b, (((1,), (1,)), ((), ())), preferred_element_type=F32)


def mm_tn(a, b):
    return lax.dot_general(a, b, (((0,), (0,)), ((), ())), preferred_element_type=F32)


def high_low(x):
    high = x.astype(BF16)
    return high, (x - high.astype(F32)).astype(BF16)


def gelu_pair(y):
    c = math.sqrt(2.0 / math.pi)
    a = 0.044715
    k = lambda v: jnp.asarray(v, y.dtype)
    y2 = y * y
    t = jnp.tanh(y * (y2 * k(8.0 * c * a) + k(2.0 * c)))
    top = t + k(1.0)
    g = y * top
    slope = top + (g - g * t) * (y2 * k(24.0 * c * a) + k(2.0 * c))
    return g, slope


def split_lanes(even, odd):
    half = even.shape[-1] // 2
    first = lax.broadcasted_iota(jnp.int32, even.shape, 1) < half
    low = jnp.where(first, even, pltpu.roll(odd, half, 1))
    high = jnp.where(first, pltpu.roll(even, half, 1), odd)
    return low, high


def mode_rows(ref, k, pairs):
    stride = 2 * MODES
    re = ref[pl.ds(k, pairs, stride=stride), :]
    im = ref[pl.ds(MODES + k, pairs, stride=stride), :]
    return jnp.concatenate(split_lanes(re, im), axis=0)


def put_mode_rows(ref, k, pairs, rows):
    stride = 2 * MODES
    re, im = split_lanes(rows[:pairs], rows[pairs:])
    ref[pl.ds(k, pairs, stride=stride), :] = re
    ref[pl.ds(MODES + k, pairs, stride=stride), :] = im


def mixer_of(upper):
    half = upper.shape[-1] // 2
    sign = jnp.where(lax.broadcasted_iota(jnp.int32, upper.shape, 1) < half, -1.0, 1.0)
    return jnp.concatenate([upper, pltpu.roll(upper, half, 1) * sign], axis=0)


def each_mode(core, mine_ref, other_ref, ch, visit):
    kept = mine_ref.shape[1] // ch

    @pl.loop(0, mine_ref.shape[0], unroll=UNROLL)
    def _(chip):
        for side, ref in enumerate((mine_ref, other_ref)):
            for i in range(kept):
                visit((chip * 2 + (core ^ side)) * kept + i, ref[chip, i * ch : (i + 1) * ch, :])


def pre_kernel(u_ref, g_ref, ana_ref, down_ref, t_ref, hc_ref):
    ch = down_ref.shape[1]
    hid = down_ref.shape[0]
    for i in range(u_ref.shape[0]):
        t_ref[i] = mm(u_ref[i], ana_ref[...]).T
        for b in range(2):
            hc_ref[i, b * hid : (b + 1) * hid] = mm(
                down_ref[...], g_ref[i, b * ch : (b + 1) * ch]
            ).astype(BF16)


def main_kernel(
    core_ref, t_ref, mine_ref, other_ref, u_ref, g_ref, hc_ref, skip_t_ref, up_t_ref, up_ref,
    down_t_ref, syn_ref,
    res_ref, pg_ref, pay_ref, c_ref,
    m_ref, gu_ref, gd_ref, gs_ref,
):
    q = pl.program_id(0)
    steps = pl.num_programs(0)
    n_pairs = t_ref.shape[0] // (2 * MODES)
    per_step = u_ref.shape[0]
    length_x = u_ref.shape[-1]
    ch, hid = up_ref.shape

    @pl.when(q == 0)
    def _():
        gu_ref[...] = jnp.zeros_like(gu_ref)
        gd_ref[...] = jnp.zeros_like(gd_ref)
        gs_ref[...] = jnp.zeros_like(gs_ref)

        def visit(k, upper):
            rows, rows_low = high_low(mode_rows(t_ref, k, n_pairs))
            mixer, mixer_low = high_low(mixer_of(upper))
            mixed = mm(
                jnp.concatenate([rows, rows_low], axis=1), jnp.concatenate([mixer, mixer], axis=0)
            )
            put_mode_rows(m_ref, k, n_pairs, mixed + mm(rows, mixer_low))

        each_mode(core_ref[0], mine_ref, other_ref, ch, visit)

    up_t, up, down_t = up_t_ref[...], up_ref[...], down_t_ref[...]
    chunks = length_x // CHUNK
    n = per_step * chunks * 2
    span = lambda j: slice(j % chunks * CHUNK, (j % chunks + 1) * CHUNK)
    lane = lambda b: slice(b * ch, (b + 1) * ch)
    unit = lambda b: slice(b * hid, (b + 1) * hid)
    lhs_pre, pre, acts, hps, hids, outs, grads, accs = {}, {}, {}, {}, {}, {}, {}, {}
    total = {}

    def add(where, key, value):
        where[key] = where[key] + value if key in where else value

    def base(p):
        return pl.multiple_of((q * per_step + p) * (2 * MODES), 2 * MODES)

    def table_rows(j):
        return jnp.concatenate([u_ref[j // chunks, :, span(j)], syn_ref[:, span(j)]], axis=0)

    def first(j):
        p = j // chunks
        if j % chunks == 0:
            mixed, mixed_low = high_low(m_ref[pl.ds(base(p), 2 * MODES), :].T * 0.5)
            lhs_pre[p] = jnp.concatenate([skip_t_ref[...], mixed, mixed_low], axis=1)
        rhs = jnp.concatenate([table_rows(j), syn_ref[:, span(j)]], axis=0)
        pre[j] = mm(lhs_pre[p], rhs)

    def gelu_act(j):
        act, slope = gelu_pair(pre.pop(j))
        acts[j] = (act.astype(BF16), slope)

    def widen(i):
        j, b = divmod(i, 2)
        hps[i] = mm(up_t, acts[j][0][lane(b)]).astype(BF16)

    def gelu_hidden(i):
        j, b = divmod(i, 2)
        hidden, slope = gelu_pair(hps.pop(i))
        hids[i] = (hidden, hc_ref[j // chunks, unit(b), span(j)] * slope)

    def narrow(i):
        j, b = divmod(i, 2)
        hidden, hgrad = hids.pop(i)
        outs[i] = mm(down_t, hidden)
        grads[i] = mm(up, hgrad)
        add(total, "gd", mm_nt(g_ref[j // chunks, lane(b), span(j)], hidden))
        add(total, "gu", mm_nt(acts[j][0][lane(b)], hgrad))

    def last(j):
        p = j // chunks
        out = jnp.concatenate([outs.pop(2 * j), outs.pop(2 * j + 1)], axis=0)
        res_ref[p, :, span(j)] = out.astype(BF16)
        both = jnp.concatenate([grads.pop(2 * j), grads.pop(2 * j + 1)], axis=0)
        pg = (both * acts.pop(j)[1]).astype(BF16)
        pg_ref[p, :, span(j)] = pg
        add(accs, p, mm_nt(table_rows(j), pg))
        if j % chunks == chunks - 1:
            acc = accs.pop(p)
            add(total, "gs", acc[: 2 * ch])
            c_ref[pl.ds(base(p), 2 * MODES), :] = acc[2 * ch :]

    ahead = SKEW * 2
    for i in range(-ahead, n + 2):
        j, b = divmod(i + ahead, 2)
        if b == 0 and 0 <= j < n // 2:
            first(j)
            gelu_act(j)
        if 0 <= i + 1 < n:
            widen(i + 1)
        if 0 <= i < n:
            gelu_hidden(i)
        if 0 <= i - 1 < n:
            narrow(i - 1)
            if (i - 1) % 2 == 1:
                last((i - 1) // 2)
    gu_ref[...] += total["gu"]
    gd_ref[...] += total["gd"]
    gs_ref[...] += total["gs"]

    @pl.when(q == steps - 1)
    def _():
        chips = pay_ref.shape[1]
        kept = MODES // (2 * chips)
        sign = jnp.where(lax.broadcasted_iota(jnp.int32, (ch, 2 * ch), 1) < ch, 1.0, -1.0)

        @pl.loop(0, chips, unroll=UNROLL)
        def _(chip):
            for core in range(2):
                for i in range(kept):
                    k = (chip * 2 + core) * kept + i
                    spec = mode_rows(t_ref, k, n_pairs).astype(BF16)
                    coef = mode_rows(c_ref, k, n_pairs).astype(BF16)
                    moment = mm_tn(spec, coef)
                    grad = moment[:ch] + pltpu.roll(moment[ch:], ch, 1) * sign
                    pay_ref[core, chip, i * ch : (i + 1) * ch, :] = grad

        at = kept * ch
        part = ch // chips
        skip = gs_ref[:ch] + pltpu.roll(gs_ref[ch:], ch, 1)
        small = ch // (2 * chips)
        for o in range(2 * chips):
            chip, core = divmod(o, 2)
            side, row = divmod(o, chips)
            lanes = slice(side * 2 * ch, (side + 1) * 2 * ch)
            rows = slice(row * part, (row + 1) * part)
            pay_ref[core, chip, at : at + part, :] = gu_ref[rows, lanes]
            pay_ref[core, chip, at + part : at + 2 * part, :] = gd_ref[rows, lanes]
            tail = jnp.concatenate(
                [skip[o * small : (o + 1) * small], jnp.zeros((8 - small, 2 * ch), F32)], axis=0
            )
            pay_ref[core, chip, at + 2 * part : at + 2 * part + 8, :] = tail


def final_kernel(core_ref, c_ref, mine_ref, other_ref, pg_ref, skip_ref, ana_ref, out_ref, b_ref):
    q = pl.program_id(0)
    n_pairs = c_ref.shape[0] // (2 * MODES)
    per_step = pg_ref.shape[0]

    @pl.when(q == 0)
    def _():
        def visit(k, upper):
            coef = mode_rows(c_ref, k, n_pairs).astype(BF16)
            put_mode_rows(b_ref, k, n_pairs, mm_nt(coef, mixer_of(upper).astype(BF16)))

        each_mode(core_ref[0], mine_ref, other_ref, skip_ref.shape[0] // 2, visit)

    for p in range(per_step):
        base = pl.multiple_of((q * per_step + p) * (2 * MODES), 2 * MODES)
        back, back_low = high_low(b_ref[pl.ds(base, 2 * MODES), :].T)
        lhs = jnp.concatenate([skip_ref[...], back, back_low], axis=1)
        rhs = jnp.concatenate([pg_ref[p], ana_ref[...], ana_ref[...]], axis=0)
        out_ref[p] = mm(lhs, rhs).astype(BF16)


def twice(weight):
    zeros = jnp.zeros_like(weight)
    upper = jnp.concatenate([weight, zeros], axis=1)
    lower = jnp.concatenate([zeros, weight], axis=1)
    return jnp.concatenate([upper, lower], axis=0)


def whole(shape):
    return pl.BlockSpec(shape, lambda *_: (0,) * len(shape))


def local(fields, spec_weight, skip_weight, up_weight, down_weight, cotangent):
    length_x, count_y, count_z, ch = fields.shape
    hid = up_weight.shape[1]
    pencils = count_y * count_z
    pairs = pencils // 2
    owners = lax.axis_size("gz")
    rows_y = lax.axis_size("gy")
    chips = owners // 2
    kept = MODES // owners
    analysis, synthesis = fourier_tables(length_x, MODES)
    u = fields.transpose(1, 2, 3, 0).reshape(pairs, 2 * ch, length_x)
    g = cotangent.transpose(1, 2, 3, 0).reshape(pairs, 2 * ch, length_x)
    core = lax.axis_index("gz") % 2
    core_word = jnp.full((1,), core, jnp.int32)
    same_core = [[i for i in range(owners) if i % 2 == c] for c in range(2)]
    columns = [[i for i in range(rows_y) if i % 2 == c] for c in range(2)]

    upper = jnp.concatenate([spec_weight[:, 0], spec_weight[:, 1]], axis=2)
    mine = to_group(upper.reshape(kept * ch, 2 * ch), "gz", same_core)
    other = swapped(mine, "gz", 1)

    def big(n, rows=2 * ch):
        return pl.BlockSpec((n, rows, length_x), lambda i: (i, 0, 0))

    rows = pairs * 2 * MODES
    cells = pencils * length_x
    half = BF16(0.5)
    spectra, hidden_cot = pl.pallas_call(
        pre_kernel,
        grid=(pairs // PRE_STEP,),
        in_specs=[big(PRE_STEP), big(PRE_STEP), whole((length_x, 2 * MODES)), whole((hid, ch))],
        out_specs=[
            pl.BlockSpec((PRE_STEP, 2 * MODES, 2 * ch), lambda i: (i, 0, 0)),
            big(PRE_STEP, 2 * hid),
        ],
        out_shape=[
            jax.ShapeDtypeStruct((pairs, 2 * MODES, 2 * ch), F32),
            jax.ShapeDtypeStruct((pairs, 2 * hid, length_x), BF16),
        ],
        cost_estimate=pl.CostEstimate(
            flops=2 * cells * ch * (hid + 2 * MODES), bytes_accessed=cells * 12 * ch, transcendentals=0
        ),
        name="pre",
    )(u, g, analysis, down_weight * half)
    spectra = spectra.reshape(rows, 2 * ch)

    wide = kept * ch + 2 * (2 * ch // owners) + 8
    smem = pl.BlockSpec(memory_space=pltpu.SMEM)
    weights = whole((chips, kept * ch, 2 * ch))
    result, pre_grad, payload, coeffs = pl.pallas_call(
        main_kernel,
        grid=(pairs // PER_STEP,),
        in_specs=[
            smem,
            whole((rows, 2 * ch)),
            weights,
            weights,
            big(PER_STEP),
            big(PER_STEP),
            big(PER_STEP, 2 * hid),
            whole((2 * ch, 2 * ch)),
            whole((hid, ch)),
            whole((ch, hid)),
            whole((ch, hid)),
            whole((2 * MODES, length_x)),
        ],
        out_specs=[big(PER_STEP), big(PER_STEP), whole((2, chips, wide, 2 * ch)), whole((rows, 2 * ch))],
        out_shape=[
            jax.ShapeDtypeStruct((pairs, 2 * ch, length_x), BF16),
            jax.ShapeDtypeStruct((pairs, 2 * ch, length_x), BF16),
            jax.ShapeDtypeStruct((2, chips, wide, 2 * ch), F32),
            jax.ShapeDtypeStruct((rows, 2 * ch), F32),
        ],
        scratch_shapes=[
            pltpu.VMEM((rows, 2 * ch), F32),
            pltpu.VMEM((ch, hid), F32),
            pltpu.VMEM((ch, hid), F32),
            pltpu.VMEM((2 * ch, 2 * ch), F32),
        ],
        cost_estimate=pl.CostEstimate(
            flops=16 * cells * ch * hid, bytes_accessed=cells * 16 * ch, transcendentals=cells * hid
        ),
        name="main",
    )(
        core_word, spectra, mine, other, u, g, hidden_cot, twice(skip_weight.T) * half,
        up_weight.T * half, up_weight * half, down_weight.T, synthesis.T,
    )

    kept_half = lax.dynamic_index_in_dim(payload, core, 0, keepdims=False)
    sent_half = lax.dynamic_index_in_dim(payload, 1 - core, 0, keepdims=False)
    chip_sum = kept_half + swapped(sent_half, "gz", 1)
    arrived = lax.all_to_all(chip_sum, "gz", 0, 0, axis_index_groups=same_core, tiled=True)

    grad_fields = pl.pallas_call(
        final_kernel,
        grid=(pairs // FINAL_STEP,),
        in_specs=[
            smem,
            whole((rows, 2 * ch)),
            weights,
            weights,
            big(FINAL_STEP),
            whole((2 * ch, 2 * ch)),
            whole((2 * MODES, length_x)),
        ],
        out_specs=big(FINAL_STEP),
        out_shape=jax.ShapeDtypeStruct((pairs, 2 * ch, length_x), BF16),
        scratch_shapes=[pltpu.VMEM((rows, 2 * ch), F32)],
        cost_estimate=pl.CostEstimate(
            flops=8 * cells * ch * ch, bytes_accessed=cells * 4 * ch, transcendentals=0
        ),
        name="final",
    )(core_word, coeffs, mine, other, pre_grad, twice(skip_weight), analysis.T)

    total = jnp.sum(arrived, axis=0)
    total = total + swapped(total, "gy", 1)
    total = jnp.sum(to_group(total, "gy", columns), axis=0)
    all_pencils = pencils * rows_y * owners
    cell_scale = 1.0 / math.sqrt(length_x * all_pencils)
    pencil_scale = 1.0 / math.sqrt(all_pencils)
    at = kept * ch
    part = 2 * ch // owners
    grad_spec = total[:at].reshape(kept, ch, 2, ch).transpose(0, 2, 1, 3) * pencil_scale
    small = to_group(total[at:] * cell_scale, "gz", [list(range(owners))])

    def joined(block):
        return block.reshape(2, ch, 2 * ch).transpose(1, 0, 2).reshape(ch, hid)

    grad_up = joined(small[:, :part])
    grad_down = joined(small[:, part : 2 * part]).T
    grad_skip = small[:, 2 * part : 2 * part + ch // owners, :ch].reshape(ch, ch)

    def unpacked(x):
        return x.reshape(count_y, count_z, ch, length_x).transpose(3, 0, 1, 2)

    return (unpacked(result), unpacked(grad_fields), grad_spec, grad_skip, grad_up, grad_down)


def solution(mesh):
    big = P(None, "gy", "gz", None)
    modes = P("gz", None, None, None)

    return jax.shard_map(
        local,
        mesh=mesh,
        in_specs=(big, modes, P(), P(), P(), big),
        out_specs=(big, big, modes, P(), P(), P()),
        check_vma=False,
    )
```

```python
import math

import jax
import jax.numpy as jnp
import numpy as np
from jax import lax
from jax.experimental import pallas as pl
from jax.experimental.pallas import tpu as pltpu
from jax.sharding import PartitionSpec as P

MODES = 32
BF16 = jnp.bfloat16
F32 = jnp.float32
CHUNK = 256
PER_STEP = 2
FINAL_STEP = 4
PRE_STEP = 4
PRE_CHUNK = 1024
SKEW = 2
UNROLL = 2


def to_group(block, axis, groups):
    peers = len(groups[0])
    return lax.all_to_all(
        jnp.broadcast_to(block[None], (peers, *block.shape)),
        axis, 0, 0, axis_index_groups=groups, tiled=True,
    )


def swapped(block, axis, mask):
    return lax.ppermute(block, axis, [(i, i ^ mask) for i in range(lax.axis_size(axis))])


def fourier_tables(length_x, kept):
    phase = np.outer(np.arange(length_x), np.arange(kept)) % length_x * (2.0 * np.pi / length_x)
    table = np.concatenate([np.cos(phase), -np.sin(phase)], axis=1) / math.sqrt(length_x)
    doubled = np.where(np.arange(2 * kept) % kept == 0, 1.0, 2.0)
    return table.astype(BF16), (table * doubled).astype(BF16)


def mm(a, b):
    return jnp.dot(a, b, preferred_element_type=F32)


def mm_nt(a, b):
    return lax.dot_general(a, b, (((1,), (1,)), ((), ())), preferred_element_type=F32)


def mm_tn(a, b):
    return lax.dot_general(a, b, (((0,), (0,)), ((), ())), preferred_element_type=F32)


def high_low(x):
    high = x.astype(BF16)
    return high, (x - high.astype(F32)).astype(BF16)


def gelu_pair(y):
    c = math.sqrt(2.0 / math.pi)
    a = 0.044715
    k = lambda v: jnp.asarray(v, y.dtype)
    y2 = y * y
    t = jnp.tanh(y * (y2 * k(8.0 * c * a) + k(2.0 * c)))
    top = t + k(1.0)
    g = y * top
    slope = top + (g - g * t) * (y2 * k(24.0 * c * a) + k(2.0 * c))
    return g, slope


def split_lanes(even, odd):
    half = even.shape[-1] // 2
    first = lax.broadcasted_iota(jnp.int32, even.shape, 1) < half
    low = jnp.where(first, even, pltpu.roll(odd, half, 1))
    high = jnp.where(first, pltpu.roll(even, half, 1), odd)
    return low, high


def mode_rows(ref, k, pairs):
    stride = 2 * MODES
    re = ref[pl.ds(k, pairs, stride=stride), :]
    im = ref[pl.ds(MODES + k, pairs, stride=stride), :]
    return jnp.concatenate(split_lanes(re, im), axis=0)


def put_mode_rows(ref, k, pairs, rows):
    stride = 2 * MODES
    re, im = split_lanes(rows[:pairs], rows[pairs:])
    ref[pl.ds(k, pairs, stride=stride), :] = re
    ref[pl.ds(MODES + k, pairs, stride=stride), :] = im


def mixer_of(upper):
    half = upper.shape[-1] // 2
    sign = jnp.where(lax.broadcasted_iota(jnp.int32, upper.shape, 1) < half, -1.0, 1.0)
    return jnp.concatenate([upper, pltpu.roll(upper, half, 1) * sign], axis=0)


def each_mode(core, mine_ref, other_ref, ch, visit):
    kept = mine_ref.shape[1] // ch

    @pl.loop(0, mine_ref.shape[0], unroll=UNROLL)
    def _(chip):
        for side, ref in enumerate((mine_ref, other_ref)):
            for i in range(kept):
                visit((chip * 2 + (core ^ side)) * kept + i, ref[chip, i * ch : (i + 1) * ch, :])


def pre_kernel(u_ref, g_ref, ana_ref, down_t_ref, t_ref, hc_ref):
    ch, hid = down_t_ref.shape
    length_x = u_ref.shape[-1]
    down = down_t_ref[...].T * BF16(0.5)
    for i in range(u_ref.shape[0]):
        t_ref[i] = mm(u_ref[i], ana_ref[...]).T
        for j in range(length_x // PRE_CHUNK):
            span = slice(j * PRE_CHUNK, (j + 1) * PRE_CHUNK)
            for b in range(2):
                hc = mm(down, g_ref[i, b * ch : (b + 1) * ch, span])
                hc_ref[i, b * hid : (b + 1) * hid, span] = hc.astype(BF16)


def main_kernel(
    core_ref, t_ref, mine_ref, other_ref, u_ref, g_ref, hc_ref, skip_t_ref, up_t_ref, up_ref,
    down_t_ref, syn_ref,
    res_ref, pg_ref, kept_ref, sent_ref, c_ref,
    m_ref, gu_ref, gd_ref, gs_ref,
):
    q = pl.program_id(0)
    steps = pl.num_programs(0)
    n_pairs = t_ref.shape[0] // (2 * MODES)
    per_step = u_ref.shape[0]
    length_x = u_ref.shape[-1]
    ch, hid = up_ref.shape

    @pl.when(q == 0)
    def _():
        gu_ref[...] = jnp.zeros_like(gu_ref)
        gd_ref[...] = jnp.zeros_like(gd_ref)
        gs_ref[...] = jnp.zeros_like(gs_ref)

        def visit(k, upper):
            rows, rows_low = high_low(mode_rows(t_ref, k, n_pairs))
            mixer, mixer_low = high_low(mixer_of(upper))
            mixed = mm(
                jnp.concatenate([rows, rows_low], axis=1), jnp.concatenate([mixer, mixer], axis=0)
            )
            put_mode_rows(m_ref, k, n_pairs, mixed + mm(rows, mixer_low))

        each_mode(core_ref[0], mine_ref, other_ref, ch, visit)

    up_t, up, down_t = up_t_ref[...], up_ref[...], down_t_ref[...]
    chunks = length_x // CHUNK
    n = per_step * chunks * 2
    span = lambda j: slice(j % chunks * CHUNK, (j % chunks + 1) * CHUNK)
    lane = lambda b: slice(b * ch, (b + 1) * ch)
    unit = lambda b: slice(b * hid, (b + 1) * hid)
    lhs_pre, pre, acts, hps, hids, outs, grads, accs = {}, {}, {}, {}, {}, {}, {}, {}
    total = {}

    def add(where, key, value):
        where[key] = where[key] + value if key in where else value

    def base(p):
        return pl.multiple_of((q * per_step + p) * (2 * MODES), 2 * MODES)

    def table_rows(j):
        return jnp.concatenate([u_ref[j // chunks, :, span(j)], syn_ref[:, span(j)]], axis=0)

    def first(j):
        p = j // chunks
        if j % chunks == 0:
            mixed, mixed_low = high_low(m_ref[pl.ds(base(p), 2 * MODES), :].T * 0.5)
            lhs_pre[p] = jnp.concatenate([skip_t_ref[...], mixed, mixed_low], axis=1)
        rhs = jnp.concatenate([table_rows(j), syn_ref[:, span(j)]], axis=0)
        pre[j] = mm(lhs_pre[p], rhs)

    def gelu_act(j):
        act, slope = gelu_pair(pre.pop(j))
        acts[j] = (act.astype(BF16), slope)

    def widen(i):
        j, b = divmod(i, 2)
        hps[i] = mm(up_t, acts[j][0][lane(b)]).astype(BF16)

    def gelu_hidden(i):
        j, b = divmod(i, 2)
        hidden, slope = gelu_pair(hps.pop(i))
        hids[i] = (hidden, hc_ref[j // chunks, unit(b), span(j)] * slope)

    def narrow(i):
        j, b = divmod(i, 2)
        hidden, hgrad = hids.pop(i)
        outs[i] = mm(down_t, hidden)
        grads[i] = mm(up, hgrad)
        add(total, "gd", mm_nt(g_ref[j // chunks, lane(b), span(j)], hidden))
        add(total, "gu", mm_nt(acts[j][0][lane(b)], hgrad))

    def last(j):
        p = j // chunks
        out = jnp.concatenate([outs.pop(2 * j), outs.pop(2 * j + 1)], axis=0)
        res_ref[p, :, span(j)] = out.astype(BF16)
        both = jnp.concatenate([grads.pop(2 * j), grads.pop(2 * j + 1)], axis=0)
        pg = (both * acts.pop(j)[1]).astype(BF16)
        pg_ref[p, :, span(j)] = pg
        add(accs, p, mm_nt(table_rows(j), pg))
        if j % chunks == chunks - 1:
            acc = accs.pop(p)
            add(total, "gs", acc[: 2 * ch])
            c_ref[pl.ds(base(p), 2 * MODES), :] = acc[2 * ch :]

    ahead = SKEW * 2
    for i in range(-ahead, n + 2):
        j, b = divmod(i + ahead, 2)
        if b == 0 and 0 <= j < n // 2:
            first(j)
            gelu_act(j)
        if 0 <= i + 1 < n:
            widen(i + 1)
        if 0 <= i < n:
            gelu_hidden(i)
        if 0 <= i - 1 < n:
            narrow(i - 1)
            if (i - 1) % 2 == 1:
                last((i - 1) // 2)
    gu_ref[...] += total["gu"]
    gd_ref[...] += total["gd"]
    gs_ref[...] += total["gs"]

    @pl.when(q == steps - 1)
    def _():
        chips = kept_ref.shape[0]
        kept = MODES // (2 * chips)
        mine = core_ref[0]
        sign = jnp.where(lax.broadcasted_iota(jnp.int32, (ch, 2 * ch), 1) < ch, 1.0, -1.0)

        @pl.loop(0, chips, unroll=UNROLL)
        def _(chip):
            for side, ref in enumerate((kept_ref, sent_ref)):
                for i in range(kept):
                    k = (chip * 2 + (mine ^ side)) * kept + i
                    spec = mode_rows(t_ref, k, n_pairs).astype(BF16)
                    coef = mode_rows(c_ref, k, n_pairs).astype(BF16)
                    moment = mm_tn(spec, coef)
                    grad = moment[:ch] + pltpu.roll(moment[ch:], ch, 1) * sign
                    ref[chip, i * ch : (i + 1) * ch, :] = grad

        at = kept * ch
        part = ch // chips
        gs_ref[:ch] += pltpu.roll(gs_ref[ch:], ch, 1)
        small = ch // (2 * chips)
        for chip in range(chips):
            half_at = slice(chip // (chips // 2) * 2 * ch, (chip // (chips // 2) + 1) * 2 * ch)
            for side, ref in enumerate((kept_ref, sent_ref)):
                o = chip * 2 + (mine ^ side)
                rows = pl.ds(pl.multiple_of(o % chips * part, part), part)
                ref[chip, at : at + part, :] = gu_ref[rows, half_at]
                ref[chip, at + part : at + 2 * part, :] = gd_ref[rows, half_at]
                ref[chip, at + 2 * part : at + 2 * part + 8, :] = jnp.zeros((8, 2 * ch), F32)
                ref[chip, at + 2 * part : at + 2 * part + small, :] = gs_ref[pl.ds(o * small, small), :]


def final_kernel(core_ref, c_ref, mine_ref, other_ref, pg_ref, skip_ref, ana_ref, out_ref, b_ref):
    q = pl.program_id(0)
    n_pairs = c_ref.shape[0] // (2 * MODES)
    per_step = pg_ref.shape[0]

    @pl.when(q == 0)
    def _():
        def visit(k, upper):
            coef = mode_rows(c_ref, k, n_pairs).astype(BF16)
            put_mode_rows(b_ref, k, n_pairs, mm_nt(coef, mixer_of(upper).astype(BF16)))

        each_mode(core_ref[0], mine_ref, other_ref, skip_ref.shape[0] // 2, visit)

    for p in range(per_step):
        base = pl.multiple_of((q * per_step + p) * (2 * MODES), 2 * MODES)
        back, back_low = high_low(b_ref[pl.ds(base, 2 * MODES), :].T)
        lhs = jnp.concatenate([skip_ref[...], back, back_low], axis=1)
        rhs = jnp.concatenate([pg_ref[p], ana_ref[...], ana_ref[...]], axis=0)
        out_ref[p] = mm(lhs, rhs).astype(BF16)


def twice(weight):
    zeros = jnp.zeros_like(weight)
    upper = jnp.concatenate([weight, zeros], axis=1)
    lower = jnp.concatenate([zeros, weight], axis=1)
    return jnp.concatenate([upper, lower], axis=0)


def whole(shape):
    return pl.BlockSpec(shape, lambda *_: (0,) * len(shape))


def local(fields, spec_weight, skip_weight, up_weight, down_weight, cotangent):
    length_x, count_y, count_z, ch = fields.shape
    hid = up_weight.shape[1]
    pencils = count_y * count_z
    pairs = pencils // 2
    owners = lax.axis_size("gz")
    rows_y = lax.axis_size("gy")
    chips = owners // 2
    kept = MODES // owners
    analysis, synthesis = fourier_tables(length_x, MODES)
    u = fields.transpose(1, 2, 3, 0).reshape(pairs, 2 * ch, length_x)
    g = cotangent.transpose(1, 2, 3, 0).reshape(pairs, 2 * ch, length_x)
    core = lax.axis_index("gz") % 2
    core_word = jnp.full((1,), core, jnp.int32)
    same_core = [[i for i in range(owners) if i % 2 == c] for c in range(2)]

    upper = jnp.concatenate([spec_weight[:, 0], spec_weight[:, 1]], axis=2)
    mine = to_group(upper.reshape(kept * ch, 2 * ch), "gz", same_core)
    other = swapped(mine, "gz", 1)

    def big(n, rows=2 * ch):
        return pl.BlockSpec((n, rows, length_x), lambda i: (i, 0, 0))

    rows = pairs * 2 * MODES
    cells = pencils * length_x
    half = BF16(0.5)
    spectra, hidden_cot = pl.pallas_call(
        pre_kernel,
        grid=(pairs // PRE_STEP,),
        in_specs=[big(PRE_STEP), big(PRE_STEP), whole((length_x, 2 * MODES)), whole((ch, hid))],
        out_specs=[
            pl.BlockSpec((PRE_STEP, 2 * MODES, 2 * ch), lambda i: (i, 0, 0)),
            big(PRE_STEP, 2 * hid),
        ],
        out_shape=[
            jax.ShapeDtypeStruct((pairs, 2 * MODES, 2 * ch), F32),
            jax.ShapeDtypeStruct((pairs, 2 * hid, length_x), BF16),
        ],
        cost_estimate=pl.CostEstimate(
            flops=2 * cells * ch * (hid + 2 * MODES), bytes_accessed=cells * 12 * ch, transcendentals=0
        ),
        name="pre",
    )(u, g, analysis, down_weight.T)
    spectra = spectra.reshape(rows, 2 * ch)

    wide = kept * ch + 2 * (2 * ch // owners) + 8
    smem = pl.BlockSpec(memory_space=pltpu.SMEM)
    weights = whole((chips, kept * ch, 2 * ch))
    result, pre_grad, kept_half, sent_half, coeffs = pl.pallas_call(
        main_kernel,
        grid=(pairs // PER_STEP,),
        in_specs=[
            smem,
            whole((rows, 2 * ch)),
            weights,
            weights,
            big(PER_STEP),
            big(PER_STEP),
            big(PER_STEP, 2 * hid),
            whole((2 * ch, 2 * ch)),
            whole((hid, ch)),
            whole((ch, hid)),
            whole((ch, hid)),
            whole((2 * MODES, length_x)),
        ],
        out_specs=[big(PER_STEP), big(PER_STEP)]
        + [whole((chips, wide, 2 * ch))] * 2
        + [whole((rows, 2 * ch))],
        out_shape=[
            jax.ShapeDtypeStruct((pairs, 2 * ch, length_x), BF16),
            jax.ShapeDtypeStruct((pairs, 2 * ch, length_x), BF16),
            jax.ShapeDtypeStruct((chips, wide, 2 * ch), F32),
            jax.ShapeDtypeStruct((chips, wide, 2 * ch), F32),
            jax.ShapeDtypeStruct((rows, 2 * ch), F32),
        ],
        scratch_shapes=[
            pltpu.VMEM((rows, 2 * ch), F32),
            pltpu.VMEM((ch, hid), F32),
            pltpu.VMEM((ch, hid), F32),
            pltpu.VMEM((2 * ch, 2 * ch), F32),
        ],
        cost_estimate=pl.CostEstimate(
            flops=16 * cells * ch * hid, bytes_accessed=cells * 16 * ch, transcendentals=cells * hid
        ),
        name="main",
    )(
        core_word, spectra, mine, other, u, g, hidden_cot, twice(skip_weight.T) * half,
        up_weight.T * half, up_weight * half, down_weight.T, synthesis.T,
    )

    chip_sum = kept_half + swapped(sent_half, "gz", 1)
    arrived = lax.all_to_all(chip_sum, "gz", 0, 0, axis_index_groups=same_core, tiled=True)

    grad_fields = pl.pallas_call(
        final_kernel,
        grid=(pairs // FINAL_STEP,),
        in_specs=[
            smem,
            whole((rows, 2 * ch)),
            weights,
            weights,
            big(FINAL_STEP),
            whole((2 * ch, 2 * ch)),
            whole((2 * MODES, length_x)),
        ],
        out_specs=big(FINAL_STEP),
        out_shape=jax.ShapeDtypeStruct((pairs, 2 * ch, length_x), BF16),
        scratch_shapes=[pltpu.VMEM((rows, 2 * ch), F32)],
        cost_estimate=pl.CostEstimate(
            flops=8 * cells * ch * ch, bytes_accessed=cells * 4 * ch, transcendentals=0
        ),
        name="final",
    )(core_word, coeffs, mine, other, pre_grad, twice(skip_weight), analysis.T)

    total = jnp.sum(arrived, axis=0)
    all_pencils = pencils * rows_y * owners
    cell_scale = 1.0 / math.sqrt(length_x * all_pencils)
    pencil_scale = 1.0 / math.sqrt(all_pencils)
    at = kept * ch
    part = 2 * ch // owners
    everyone = lambda axis: [list(range(lax.axis_size(axis)))]
    small = to_group(total[at:], "gy", everyone("gy"))
    spec = total[:at]
    spec = spec + swapped(spec, "gy", 1)
    small = jnp.sum(small, axis=0) * cell_scale
    small = to_group(small, "gz", everyone("gz"))
    spec = (spec + swapped(spec, "gy", 2) + swapped(spec, "gy", 4) + swapped(spec, "gy", 6)) * pencil_scale
    grad_spec = spec.reshape(kept, ch, 2, ch).transpose(0, 2, 1, 3)

    def joined(block):
        return block.reshape(2, ch, 2 * ch).transpose(1, 0, 2).reshape(ch, hid)

    grad_up = joined(small[:, :part])
    grad_down = joined(small[:, part : 2 * part]).T
    grad_skip = small[:, 2 * part : 2 * part + ch // owners, :ch].reshape(ch, ch)

    def unpacked(x):
        return x.reshape(count_y, count_z, ch, length_x).transpose(3, 0, 1, 2)

    return (unpacked(result), unpacked(grad_fields), grad_spec, grad_skip, grad_up, grad_down)


def solution(mesh):
    big = P(None, "gy", "gz", None)
    modes = P("gz", None, None, None)

    return jax.shard_map(
        local,
        mesh=mesh,
        in_specs=(big, modes, P(), P(), P(), big),
        out_specs=(big, big, modes, P(), P(), P()),
        check_vma=False,
    )
```

```python
import math

import jax
import jax.numpy as jnp
import numpy as np
from jax import lax
from jax.experimental import pallas as pl
from jax.experimental.pallas import tpu as pltpu
from jax.sharding import PartitionSpec as P

MODES = 32
BF16 = jnp.bfloat16
F32 = jnp.float32
CHUNK = 256
PER_STEP = 2
FINAL_STEP = 4
PRE_STEP = 4
PRE_CHUNK = 1024
SKEW = 2
UNROLL = 4


def to_group(block, axis, groups):
    peers = len(groups[0])
    return lax.all_to_all(
        jnp.broadcast_to(block[None], (peers, *block.shape)),
        axis, 0, 0, axis_index_groups=groups, tiled=True,
    )


def swapped(block, axis, mask):
    return lax.ppermute(block, axis, [(i, i ^ mask) for i in range(lax.axis_size(axis))])


def fourier_tables(length_x, kept):
    phase = np.outer(np.arange(length_x), np.arange(kept)) % length_x * (2.0 * np.pi / length_x)
    table = np.concatenate([np.cos(phase), -np.sin(phase)], axis=1) / math.sqrt(length_x)
    doubled = np.where(np.arange(2 * kept) % kept == 0, 1.0, 2.0)
    return table.astype(BF16), (table * doubled).astype(BF16)


def mm(a, b):
    return jnp.dot(a, b, preferred_element_type=F32)


def mm_nt(a, b):
    return lax.dot_general(a, b, (((1,), (1,)), ((), ())), preferred_element_type=F32)


def mm_tn(a, b):
    return lax.dot_general(a, b, (((0,), (0,)), ((), ())), preferred_element_type=F32)


def high_low(x):
    high = x.astype(BF16)
    return high, (x - high.astype(F32)).astype(BF16)


def gelu_pair(y):
    c = math.sqrt(2.0 / math.pi)
    a = 0.044715
    k = lambda v: jnp.asarray(v, y.dtype)
    y2 = y * y
    t = jnp.tanh(y * (y2 * k(8.0 * c * a) + k(2.0 * c)))
    top = t + k(1.0)
    g = y * top
    slope = top + (g - g * t) * (y2 * k(24.0 * c * a) + k(2.0 * c))
    return g, slope


def split_lanes(even, odd):
    half = even.shape[-1] // 2
    first = lax.broadcasted_iota(jnp.int32, even.shape, 1) < half
    low = jnp.where(first, even, pltpu.roll(odd, half, 1))
    high = jnp.where(first, pltpu.roll(even, half, 1), odd)
    return low, high


def mode_rows(ref, k, pairs):
    stride = 2 * MODES
    re = ref[pl.ds(k, pairs, stride=stride), :]
    im = ref[pl.ds(MODES + k, pairs, stride=stride), :]
    return jnp.concatenate(split_lanes(re, im), axis=0)


def put_mode_rows(ref, k, pairs, rows):
    stride = 2 * MODES
    re, im = split_lanes(rows[:pairs], rows[pairs:])
    ref[pl.ds(k, pairs, stride=stride), :] = re
    ref[pl.ds(MODES + k, pairs, stride=stride), :] = im


def mixer_of(upper):
    half = upper.shape[-1] // 2
    sign = jnp.where(lax.broadcasted_iota(jnp.int32, upper.shape, 1) < half, -1.0, 1.0)
    return jnp.concatenate([upper, pltpu.roll(upper, half, 1) * sign], axis=0)


def each_mode(core, mine_ref, other_ref, ch, visit):
    kept = mine_ref.shape[1] // ch

    @pl.loop(0, mine_ref.shape[0], unroll=UNROLL)
    def _(chip):
        for side, ref in enumerate((mine_ref, other_ref)):
            for i in range(kept):
                visit((chip * 2 + (core ^ side)) * kept + i, ref[chip, i * ch : (i + 1) * ch, :])


def copies_kernel(w_ref, out_ref):
    kept, _, ch, _ = w_ref.shape
    for i in range(kept):
        upper = jnp.concatenate([w_ref[i, 0], w_ref[i, 1]], axis=1)
        for chip in range(out_ref.shape[0]):
            out_ref[chip, i * ch : (i + 1) * ch, :] = upper


def pre_kernel(u_ref, g_ref, ana_ref, down_t_ref, t_ref, hc_ref):
    ch, hid = down_t_ref.shape
    length_x = u_ref.shape[-1]
    down = down_t_ref[...].T * BF16(0.5)
    for i in range(u_ref.shape[0]):
        t_ref[i] = mm(u_ref[i], ana_ref[...]).T
        for j in range(length_x // PRE_CHUNK):
            span = slice(j * PRE_CHUNK, (j + 1) * PRE_CHUNK)
            for b in range(2):
                hc = mm(down, g_ref[i, b * ch : (b + 1) * ch, span])
                hc_ref[i, b * hid : (b + 1) * hid, span] = hc.astype(BF16)


def main_kernel(
    core_ref, t_ref, mine_ref, other_ref, u_ref, g_ref, hc_ref, skip_ref, up_ref, down_t_ref,
    syn_ref,
    res_ref, pg_ref, kept_ref, sent_ref, c_ref,
    m_ref, gu_ref, gd_ref, gs_ref,
):
    q = pl.program_id(0)
    steps = pl.num_programs(0)
    n_pairs = t_ref.shape[0] // (2 * MODES)
    per_step = u_ref.shape[0]
    length_x = u_ref.shape[-1]
    ch, hid = up_ref.shape

    @pl.when(q == 0)
    def _():
        gu_ref[...] = jnp.zeros_like(gu_ref)
        gd_ref[...] = jnp.zeros_like(gd_ref)
        gs_ref[...] = jnp.zeros_like(gs_ref)

        def visit(k, upper):
            rows, rows_low = high_low(mode_rows(t_ref, k, n_pairs))
            mixer, mixer_low = high_low(mixer_of(upper))
            mixed = mm(
                jnp.concatenate([rows, rows_low], axis=1), jnp.concatenate([mixer, mixer], axis=0)
            )
            put_mode_rows(m_ref, k, n_pairs, mixed + mm(rows, mixer_low))

        each_mode(core_ref[0], mine_ref, other_ref, ch, visit)

    up = up_ref[...] * BF16(0.5)
    up_t, down_t = up.T, down_t_ref[...]
    skip_t = (twice(skip_ref[...].astype(F32).T) * 0.5).astype(BF16)
    chunks = length_x // CHUNK
    n = per_step * chunks * 2
    span = lambda j: slice(j % chunks * CHUNK, (j % chunks + 1) * CHUNK)
    lane = lambda b: slice(b * ch, (b + 1) * ch)
    unit = lambda b: slice(b * hid, (b + 1) * hid)
    lhs_pre, pre, acts, hps, hids, outs, grads, accs = {}, {}, {}, {}, {}, {}, {}, {}
    total = {}

    def add(where, key, value):
        where[key] = where[key] + value if key in where else value

    def base(p):
        return pl.multiple_of((q * per_step + p) * (2 * MODES), 2 * MODES)

    def table_rows(j):
        return jnp.concatenate([u_ref[j // chunks, :, span(j)], syn_ref[:, span(j)]], axis=0)

    def first(j):
        p = j // chunks
        if j % chunks == 0:
            mixed, mixed_low = high_low(m_ref[pl.ds(base(p), 2 * MODES), :].T * 0.5)
            lhs_pre[p] = jnp.concatenate([skip_t, mixed, mixed_low], axis=1)
        rhs = jnp.concatenate([table_rows(j), syn_ref[:, span(j)]], axis=0)
        pre[j] = mm(lhs_pre[p], rhs)

    def gelu_act(j):
        act, slope = gelu_pair(pre.pop(j))
        acts[j] = (act.astype(BF16), slope)

    def widen(i):
        j, b = divmod(i, 2)
        hps[i] = mm(up_t, acts[j][0][lane(b)]).astype(BF16)

    def gelu_hidden(i):
        j, b = divmod(i, 2)
        hidden, slope = gelu_pair(hps.pop(i))
        hids[i] = (hidden, hc_ref[j // chunks, unit(b), span(j)] * slope)

    def narrow(i):
        j, b = divmod(i, 2)
        hidden, hgrad = hids.pop(i)
        outs[i] = mm(down_t, hidden)
        grads[i] = mm(up, hgrad)
        add(total, "gd", mm_nt(g_ref[j // chunks, lane(b), span(j)], hidden))
        add(total, "gu", mm_nt(acts[j][0][lane(b)], hgrad))

    def last(j):
        p = j // chunks
        out = jnp.concatenate([outs.pop(2 * j), outs.pop(2 * j + 1)], axis=0)
        res_ref[p, :, span(j)] = out.astype(BF16)
        both = jnp.concatenate([grads.pop(2 * j), grads.pop(2 * j + 1)], axis=0)
        pg = (both * acts.pop(j)[1]).astype(BF16)
        pg_ref[p, :, span(j)] = pg
        add(accs, p, mm_nt(table_rows(j), pg))
        if j % chunks == chunks - 1:
            acc = accs.pop(p)
            add(total, "gs", acc[: 2 * ch])
            c_ref[pl.ds(base(p), 2 * MODES), :] = acc[2 * ch :]

    ahead = SKEW * 2
    for i in range(-ahead, n + 2):
        j, b = divmod(i + ahead, 2)
        if b == 0 and 0 <= j < n // 2:
            first(j)
            gelu_act(j)
        if 0 <= i + 1 < n:
            widen(i + 1)
        if 0 <= i < n:
            gelu_hidden(i)
        if 0 <= i - 1 < n:
            narrow(i - 1)
            if (i - 1) % 2 == 1:
                last((i - 1) // 2)
    gu_ref[...] += total["gu"]
    gd_ref[...] += total["gd"]
    gs_ref[...] += total["gs"]

    @pl.when(q == steps - 1)
    def _():
        chips = kept_ref.shape[0]
        kept = MODES // (2 * chips)
        mine = core_ref[0]
        sign = jnp.where(lax.broadcasted_iota(jnp.int32, (ch, 2 * ch), 1) < ch, 1.0, -1.0)

        @pl.loop(0, chips, unroll=UNROLL)
        def _(chip):
            for side, ref in enumerate((kept_ref, sent_ref)):
                for i in range(kept):
                    k = (chip * 2 + (mine ^ side)) * kept + i
                    spec = mode_rows(t_ref, k, n_pairs).astype(BF16)
                    coef = mode_rows(c_ref, k, n_pairs).astype(BF16)
                    moment = mm_tn(spec, coef)
                    grad = moment[:ch] + pltpu.roll(moment[ch:], ch, 1) * sign
                    ref[chip, i * ch : (i + 1) * ch, :] = grad

        at = kept * ch
        part = ch // chips
        gs_ref[:ch] += pltpu.roll(gs_ref[ch:], ch, 1)
        small = ch // (2 * chips)
        for chip in range(chips):
            half_at = slice(chip // (chips // 2) * 2 * ch, (chip // (chips // 2) + 1) * 2 * ch)
            for side, ref in enumerate((kept_ref, sent_ref)):
                o = chip * 2 + (mine ^ side)
                rows = pl.ds(pl.multiple_of(o % chips * part, part), part)
                ref[chip, at : at + part, :] = gu_ref[rows, half_at]
                ref[chip, at + part : at + 2 * part, :] = gd_ref[rows, half_at]
                ref[chip, at + 2 * part : at + 2 * part + 8, :] = jnp.zeros((8, 2 * ch), F32)
                ref[chip, at + 2 * part : at + 2 * part + small, :] = gs_ref[pl.ds(o * small, small), :]


def final_kernel(core_ref, c_ref, mine_ref, other_ref, pg_ref, skip_ref, ana_ref, out_ref, b_ref):
    q = pl.program_id(0)
    n_pairs = c_ref.shape[0] // (2 * MODES)
    per_step = pg_ref.shape[0]

    @pl.when(q == 0)
    def _():
        def visit(k, upper):
            coef = mode_rows(c_ref, k, n_pairs).astype(BF16)
            put_mode_rows(b_ref, k, n_pairs, mm_nt(coef, mixer_of(upper).astype(BF16)))

        each_mode(core_ref[0], mine_ref, other_ref, skip_ref.shape[0] // 2, visit)

    for p in range(per_step):
        base = pl.multiple_of((q * per_step + p) * (2 * MODES), 2 * MODES)
        back, back_low = high_low(b_ref[pl.ds(base, 2 * MODES), :].T)
        lhs = jnp.concatenate([skip_ref[...], back, back_low], axis=1)
        rhs = jnp.concatenate([pg_ref[p], ana_ref[...], ana_ref[...]], axis=0)
        out_ref[p] = mm(lhs, rhs).astype(BF16)


def twice(weight):
    zeros = jnp.zeros_like(weight)
    upper = jnp.concatenate([weight, zeros], axis=1)
    lower = jnp.concatenate([zeros, weight], axis=1)
    return jnp.concatenate([upper, lower], axis=0)


def whole(shape):
    return pl.BlockSpec(shape, lambda *_: (0,) * len(shape))


def local(fields, spec_weight, skip_weight, up_weight, down_weight, cotangent):
    length_x, count_y, count_z, ch = fields.shape
    hid = up_weight.shape[1]
    pencils = count_y * count_z
    pairs = pencils // 2
    owners = lax.axis_size("gz")
    rows_y = lax.axis_size("gy")
    chips = owners // 2
    kept = MODES // owners
    analysis, synthesis = fourier_tables(length_x, MODES)
    u = fields.transpose(1, 2, 3, 0).reshape(pairs, 2 * ch, length_x)
    g = cotangent.transpose(1, 2, 3, 0).reshape(pairs, 2 * ch, length_x)
    core = lax.axis_index("gz") % 2
    core_word = jnp.full((1,), core, jnp.int32)
    same_core = [[i for i in range(owners) if i % 2 == c] for c in range(2)]

    copies = pl.pallas_call(
        copies_kernel,
        out_shape=jax.ShapeDtypeStruct((chips, kept * ch, 2 * ch), F32),
        name="copies",
    )(spec_weight)
    mine = lax.all_to_all(copies, "gz", 0, 0, axis_index_groups=same_core, tiled=True)
    other = swapped(mine, "gz", 1)

    def big(n, rows=2 * ch):
        return pl.BlockSpec((n, rows, length_x), lambda i: (i, 0, 0))

    rows = pairs * 2 * MODES
    cells = pencils * length_x
    spectra, hidden_cot = pl.pallas_call(
        pre_kernel,
        grid=(pairs // PRE_STEP,),
        in_specs=[big(PRE_STEP), big(PRE_STEP), whole((length_x, 2 * MODES)), whole((ch, hid))],
        out_specs=[
            pl.BlockSpec((PRE_STEP, 2 * MODES, 2 * ch), lambda i: (i, 0, 0)),
            big(PRE_STEP, 2 * hid),
        ],
        out_shape=[
            jax.ShapeDtypeStruct((pairs, 2 * MODES, 2 * ch), F32),
            jax.ShapeDtypeStruct((pairs, 2 * hid, length_x), BF16),
        ],
        cost_estimate=pl.CostEstimate(
            flops=2 * cells * ch * (hid + 2 * MODES), bytes_accessed=cells * 12 * ch, transcendentals=0
        ),
        name="pre",
    )(u, g, analysis, down_weight.T)
    spectra = spectra.reshape(rows, 2 * ch)

    wide = kept * ch + 2 * (2 * ch // owners) + 8
    smem = pl.BlockSpec(memory_space=pltpu.SMEM)
    weights = whole((chips, kept * ch, 2 * ch))
    result, pre_grad, kept_half, sent_half, coeffs = pl.pallas_call(
        main_kernel,
        grid=(pairs // PER_STEP,),
        in_specs=[
            smem,
            whole((rows, 2 * ch)),
            weights,
            weights,
            big(PER_STEP),
            big(PER_STEP),
            big(PER_STEP, 2 * hid),
            whole((ch, ch)),
            whole((ch, hid)),
            whole((ch, hid)),
            whole((2 * MODES, length_x)),
        ],
        out_specs=[big(PER_STEP), big(PER_STEP)]
        + [whole((chips, wide, 2 * ch))] * 2
        + [whole((rows, 2 * ch))],
        out_shape=[
            jax.ShapeDtypeStruct((pairs, 2 * ch, length_x), BF16),
            jax.ShapeDtypeStruct((pairs, 2 * ch, length_x), BF16),
            jax.ShapeDtypeStruct((chips, wide, 2 * ch), F32),
            jax.ShapeDtypeStruct((chips, wide, 2 * ch), F32),
            jax.ShapeDtypeStruct((rows, 2 * ch), F32),
        ],
        scratch_shapes=[
            pltpu.VMEM((rows, 2 * ch), F32),
            pltpu.VMEM((ch, hid), F32),
            pltpu.VMEM((ch, hid), F32),
            pltpu.VMEM((2 * ch, 2 * ch), F32),
        ],
        cost_estimate=pl.CostEstimate(
            flops=16 * cells * ch * hid, bytes_accessed=cells * 16 * ch, transcendentals=cells * hid
        ),
        name="main",
    )(
        core_word, spectra, mine, other, u, g, hidden_cot, skip_weight, up_weight, down_weight.T,
        synthesis.T,
    )

    chip_sum = kept_half + swapped(sent_half, "gz", 1)
    arrived = lax.all_to_all(chip_sum, "gz", 0, 0, axis_index_groups=same_core, tiled=True)

    grad_fields = pl.pallas_call(
        final_kernel,
        grid=(pairs // FINAL_STEP,),
        in_specs=[
            smem,
            whole((rows, 2 * ch)),
            weights,
            weights,
            big(FINAL_STEP),
            whole((2 * ch, 2 * ch)),
            whole((2 * MODES, length_x)),
        ],
        out_specs=big(FINAL_STEP),
        out_shape=jax.ShapeDtypeStruct((pairs, 2 * ch, length_x), BF16),
        scratch_shapes=[pltpu.VMEM((rows, 2 * ch), F32)],
        cost_estimate=pl.CostEstimate(
            flops=8 * cells * ch * ch, bytes_accessed=cells * 4 * ch, transcendentals=0
        ),
        name="final",
    )(core_word, coeffs, mine, other, pre_grad, twice(skip_weight), analysis.T)

    total = jnp.sum(arrived, axis=0)
    all_pencils = pencils * rows_y * owners
    cell_scale = 1.0 / math.sqrt(length_x * all_pencils)
    pencil_scale = 1.0 / math.sqrt(all_pencils)
    at = kept * ch
    part = 2 * ch // owners
    everyone = lambda axis: [list(range(lax.axis_size(axis)))]
    small = to_group(total[at:], "gy", everyone("gy"))
    spec = total[:at]
    spec = spec + swapped(spec, "gy", 1)
    small = jnp.sum(small, axis=0) * cell_scale
    small = to_group(small, "gz", everyone("gz"))
    spec = (spec + swapped(spec, "gy", 2) + swapped(spec, "gy", 4) + swapped(spec, "gy", 6)) * pencil_scale
    grad_spec = spec.reshape(kept, ch, 2, ch).transpose(0, 2, 1, 3)

    def joined(block):
        return block.reshape(2, ch, 2 * ch).transpose(1, 0, 2).reshape(ch, hid)

    grad_up = joined(small[:, :part])
    grad_down = joined(small[:, part : 2 * part]).T
    grad_skip = small[:, 2 * part : 2 * part + ch // owners, :ch].reshape(ch, ch)

    def unpacked(x):
        return x.reshape(count_y, count_z, ch, length_x).transpose(3, 0, 1, 2)

    return (unpacked(result), unpacked(grad_fields), grad_spec, grad_skip, grad_up, grad_down)


def solution(mesh):
    big = P(None, "gy", "gz", None)
    modes = P("gz", None, None, None)

    return jax.shard_map(
        local,
        mesh=mesh,
        in_specs=(big, modes, P(), P(), P(), big),
        out_specs=(big, big, modes, P(), P(), P()),
        check_vma=False,
    )
```

```python
import math

import jax
import jax.numpy as jnp
import numpy as np
from jax import lax
from jax.experimental import pallas as pl
from jax.experimental.pallas import tpu as pltpu
from jax.sharding import PartitionSpec as P

MODES = 32
BF16 = jnp.bfloat16
F32 = jnp.float32
CHUNK = 256
PER_STEP = 2
FINAL_STEP = 4
PRE_STEP = 4
PRE_CHUNK = 1024
SKEW = 2
UNROLL = 4
PRE_MIB = 50
MAIN_MIB = 50
FINAL_MIB = 50


def to_group(block, axis, groups):
    peers = len(groups[0])
    return lax.all_to_all(
        jnp.broadcast_to(block[None], (peers, *block.shape)),
        axis, 0, 0, axis_index_groups=groups, tiled=True,
    )


def swapped(block, axis, mask):
    return lax.ppermute(block, axis, [(i, i ^ mask) for i in range(lax.axis_size(axis))])


def fourier_tables(length_x, kept):
    phase = np.outer(np.arange(length_x), np.arange(kept)) % length_x * (2.0 * np.pi / length_x)
    table = np.concatenate([np.cos(phase), -np.sin(phase)], axis=1) / math.sqrt(length_x)
    doubled = np.where(np.arange(2 * kept) % kept == 0, 1.0, 2.0)
    return table.astype(BF16), (table * doubled).astype(BF16)


def mm(a, b):
    return jnp.dot(a, b, preferred_element_type=F32)


def mm_nt(a, b):
    return lax.dot_general(a, b, (((1,), (1,)), ((), ())), preferred_element_type=F32)


def mm_tn(a, b):
    return lax.dot_general(a, b, (((0,), (0,)), ((), ())), preferred_element_type=F32)


def high_low(x):
    high = x.astype(BF16)
    return high, (x - high.astype(F32)).astype(BF16)


def gelu_pair(y):
    c = math.sqrt(2.0 / math.pi)
    a = 0.044715
    k = lambda v: jnp.asarray(v, y.dtype)
    y2 = y * y
    t = jnp.tanh(y * (y2 * k(8.0 * c * a) + k(2.0 * c)))
    top = t + k(1.0)
    g = y * top
    slope = top + (g - g * t) * (y2 * k(24.0 * c * a) + k(2.0 * c))
    return g, slope


def split_lanes(even, odd):
    half = even.shape[-1] // 2
    first = lax.broadcasted_iota(jnp.int32, even.shape, 1) < half
    low = jnp.where(first, even, pltpu.roll(odd, half, 1))
    high = jnp.where(first, pltpu.roll(even, half, 1), odd)
    return low, high


def mode_rows(ref, k, pairs):
    stride = 2 * MODES
    re = ref[pl.ds(k, pairs, stride=stride), :]
    im = ref[pl.ds(MODES + k, pairs, stride=stride), :]
    return jnp.concatenate(split_lanes(re, im), axis=0)


def put_mode_rows(ref, k, pairs, rows):
    stride = 2 * MODES
    re, im = split_lanes(rows[:pairs], rows[pairs:])
    ref[pl.ds(k, pairs, stride=stride), :] = re
    ref[pl.ds(MODES + k, pairs, stride=stride), :] = im


def mixer_of(upper):
    half = upper.shape[-1] // 2
    sign = jnp.where(lax.broadcasted_iota(jnp.int32, upper.shape, 1) < half, -1.0, 1.0)
    return jnp.concatenate([upper, pltpu.roll(upper, half, 1) * sign], axis=0)


def each_mode(core, mine_ref, other_ref, ch, visit):
    kept = mine_ref.shape[1] // ch

    @pl.loop(0, mine_ref.shape[0], unroll=UNROLL)
    def _(chip):
        for side, ref in enumerate((mine_ref, other_ref)):
            for i in range(kept):
                visit((chip * 2 + (core ^ side)) * kept + i, ref[chip, i * ch : (i + 1) * ch, :])


def copies_kernel(w_ref, out_ref):
    kept, _, ch, _ = w_ref.shape
    for i in range(kept):
        upper = jnp.concatenate([w_ref[i, 0], w_ref[i, 1]], axis=1)
        for chip in range(out_ref.shape[0]):
            out_ref[chip, i * ch : (i + 1) * ch, :] = upper


def pre_kernel(u_ref, g_ref, ana_ref, down_t_ref, t_ref, hc_ref):
    ch, hid = down_t_ref.shape
    length_x = u_ref.shape[-1]
    down = down_t_ref[...].T * BF16(0.5)
    for i in range(u_ref.shape[0]):
        t_ref[i] = mm(u_ref[i], ana_ref[...]).T
        for j in range(length_x // PRE_CHUNK):
            span = slice(j * PRE_CHUNK, (j + 1) * PRE_CHUNK)
            for b in range(2):
                hc = mm(down, g_ref[i, b * ch : (b + 1) * ch, span])
                hc_ref[i, b * hid : (b + 1) * hid, span] = hc.astype(BF16)


def main_kernel(
    core_ref, t_ref, mine_ref, other_ref, u_ref, g_ref, hc_ref, skip_ref, up_ref, down_t_ref,
    syn_ref,
    res_ref, pg_ref, kept_ref, sent_ref, c_ref,
    m_ref, gu_ref, gd_ref, gs_ref,
):
    q = pl.program_id(0)
    steps = pl.num_programs(0)
    n_pairs = t_ref.shape[0] // (2 * MODES)
    per_step = u_ref.shape[0]
    length_x = u_ref.shape[-1]
    ch, hid = up_ref.shape

    @pl.when(q == 0)
    def _():
        gu_ref[...] = jnp.zeros_like(gu_ref)
        gd_ref[...] = jnp.zeros_like(gd_ref)
        gs_ref[...] = jnp.zeros_like(gs_ref)

        def visit(k, upper):
            rows, rows_low = high_low(mode_rows(t_ref, k, n_pairs))
            mixer, mixer_low = high_low(mixer_of(upper))
            mixed = mm(
                jnp.concatenate([rows, rows_low], axis=1), jnp.concatenate([mixer, mixer], axis=0)
            )
            put_mode_rows(m_ref, k, n_pairs, mixed + mm(rows, mixer_low))

        each_mode(core_ref[0], mine_ref, other_ref, ch, visit)

    up = up_ref[...] * BF16(0.5)
    up_t, down_t = up.T, down_t_ref[...]
    skip_t = (twice(skip_ref[...].astype(F32).T) * 0.5).astype(BF16)
    chunks = length_x // CHUNK
    n = per_step * chunks * 2
    span = lambda j: slice(j % chunks * CHUNK, (j % chunks + 1) * CHUNK)
    lane = lambda b: slice(b * ch, (b + 1) * ch)
    unit = lambda b: slice(b * hid, (b + 1) * hid)
    lhs_pre, pre, acts, hps, hids, outs, grads, accs = {}, {}, {}, {}, {}, {}, {}, {}
    total = {}

    def add(where, key, value):
        where[key] = where[key] + value if key in where else value

    def base(p):
        return pl.multiple_of((q * per_step + p) * (2 * MODES), 2 * MODES)

    def table_rows(j):
        return jnp.concatenate([u_ref[j // chunks, :, span(j)], syn_ref[:, span(j)]], axis=0)

    def first(j):
        p = j // chunks
        if j % chunks == 0:
            mixed, mixed_low = high_low(m_ref[pl.ds(base(p), 2 * MODES), :].T * 0.5)
            lhs_pre[p] = jnp.concatenate([skip_t, mixed, mixed_low], axis=1)
        rhs = jnp.concatenate([table_rows(j), syn_ref[:, span(j)]], axis=0)
        pre[j] = mm(lhs_pre[p], rhs)

    def gelu_act(j):
        act, slope = gelu_pair(pre.pop(j))
        acts[j] = (act.astype(BF16), slope)

    def widen(i):
        j, b = divmod(i, 2)
        hps[i] = mm(up_t, acts[j][0][lane(b)]).astype(BF16)

    def gelu_hidden(i):
        j, b = divmod(i, 2)
        hidden, slope = gelu_pair(hps.pop(i))
        hids[i] = (hidden, hc_ref[j // chunks, unit(b), span(j)] * slope)

    def narrow(i):
        j, b = divmod(i, 2)
        hidden, hgrad = hids.pop(i)
        outs[i] = mm(down_t, hidden)
        grads[i] = mm(up, hgrad)
        add(total, "gd", mm_nt(g_ref[j // chunks, lane(b), span(j)], hidden))
        add(total, "gu", mm_nt(acts[j][0][lane(b)], hgrad))

    def last(j):
        p = j // chunks
        out = jnp.concatenate([outs.pop(2 * j), outs.pop(2 * j + 1)], axis=0)
        res_ref[p, :, span(j)] = out.astype(BF16)
        both = jnp.concatenate([grads.pop(2 * j), grads.pop(2 * j + 1)], axis=0)
        pg = (both * acts.pop(j)[1]).astype(BF16)
        pg_ref[p, :, span(j)] = pg
        add(accs, p, mm_nt(table_rows(j), pg))
        if j % chunks == chunks - 1:
            acc = accs.pop(p)
            add(total, "gs", acc[: 2 * ch])
            c_ref[pl.ds(base(p), 2 * MODES), :] = acc[2 * ch :]

    ahead = SKEW * 2
    for i in range(-ahead, n + 2):
        j, b = divmod(i + ahead, 2)
        if b == 0 and 0 <= j < n // 2:
            first(j)
            gelu_act(j)
        if 0 <= i + 1 < n:
            widen(i + 1)
        if 0 <= i < n:
            gelu_hidden(i)
        if 0 <= i - 1 < n:
            narrow(i - 1)
            if (i - 1) % 2 == 1:
                last((i - 1) // 2)
    gu_ref[...] += total["gu"]
    gd_ref[...] += total["gd"]
    gs_ref[...] += total["gs"]

    @pl.when(q == steps - 1)
    def _():
        chips = kept_ref.shape[0]
        kept = MODES // (2 * chips)
        mine = core_ref[0]
        sign = jnp.where(lax.broadcasted_iota(jnp.int32, (ch, 2 * ch), 1) < ch, 1.0, -1.0)

        @pl.loop(0, chips, unroll=UNROLL)
        def _(chip):
            for side, ref in enumerate((kept_ref, sent_ref)):
                for i in range(kept):
                    k = (chip * 2 + (mine ^ side)) * kept + i
                    spec = mode_rows(t_ref, k, n_pairs).astype(BF16)
                    coef = mode_rows(c_ref, k, n_pairs).astype(BF16)
                    moment = mm_tn(spec, coef)
                    grad = moment[:ch] + pltpu.roll(moment[ch:], ch, 1) * sign
                    ref[chip, i * ch : (i + 1) * ch, :] = grad

        at = kept * ch
        part = ch // chips
        gs_ref[:ch] += pltpu.roll(gs_ref[ch:], ch, 1)
        small = ch // (2 * chips)
        for chip in range(chips):
            half_at = slice(chip // (chips // 2) * 2 * ch, (chip // (chips // 2) + 1) * 2 * ch)
            for side, ref in enumerate((kept_ref, sent_ref)):
                o = chip * 2 + (mine ^ side)
                rows = pl.ds(pl.multiple_of(o % chips * part, part), part)
                ref[chip, at : at + part, :] = gu_ref[rows, half_at]
                ref[chip, at + part : at + 2 * part, :] = gd_ref[rows, half_at]
                ref[chip, at + 2 * part : at + 2 * part + 8, :] = jnp.zeros((8, 2 * ch), F32)
                ref[chip, at + 2 * part : at + 2 * part + small, :] = gs_ref[pl.ds(o * small, small), :]


def final_kernel(core_ref, c_ref, mine_ref, other_ref, pg_ref, skip_ref, ana_ref, out_ref, b_ref):
    q = pl.program_id(0)
    n_pairs = c_ref.shape[0] // (2 * MODES)
    per_step = pg_ref.shape[0]

    @pl.when(q == 0)
    def _():
        def visit(k, upper):
            coef = mode_rows(c_ref, k, n_pairs).astype(BF16)
            put_mode_rows(b_ref, k, n_pairs, mm_nt(coef, mixer_of(upper).astype(BF16)))

        each_mode(core_ref[0], mine_ref, other_ref, skip_ref.shape[0] // 2, visit)

    for p in range(per_step):
        base = pl.multiple_of((q * per_step + p) * (2 * MODES), 2 * MODES)
        back, back_low = high_low(b_ref[pl.ds(base, 2 * MODES), :].T)
        lhs = jnp.concatenate([skip_ref[...], back, back_low], axis=1)
        rhs = jnp.concatenate([pg_ref[p], ana_ref[...], ana_ref[...]], axis=0)
        out_ref[p] = mm(lhs, rhs).astype(BF16)


def twice(weight):
    zeros = jnp.zeros_like(weight)
    upper = jnp.concatenate([weight, zeros], axis=1)
    lower = jnp.concatenate([zeros, weight], axis=1)
    return jnp.concatenate([upper, lower], axis=0)


def whole(shape):
    return pl.BlockSpec(shape, lambda *_: (0,) * len(shape))


def local(fields, spec_weight, skip_weight, up_weight, down_weight, cotangent):
    length_x, count_y, count_z, ch = fields.shape
    hid = up_weight.shape[1]
    pencils = count_y * count_z
    pairs = pencils // 2
    owners = lax.axis_size("gz")
    rows_y = lax.axis_size("gy")
    chips = owners // 2
    kept = MODES // owners
    analysis, synthesis = fourier_tables(length_x, MODES)
    u = fields.transpose(1, 2, 3, 0).reshape(pairs, 2 * ch, length_x)
    g = cotangent.transpose(1, 2, 3, 0).reshape(pairs, 2 * ch, length_x)
    core = lax.axis_index("gz") % 2
    core_word = jnp.full((1,), core, jnp.int32)
    same_core = [[i for i in range(owners) if i % 2 == c] for c in range(2)]

    copies = pl.pallas_call(
        copies_kernel,
        out_shape=jax.ShapeDtypeStruct((chips, kept * ch, 2 * ch), F32),
        name="copies",
    )(spec_weight)
    mine = lax.all_to_all(copies, "gz", 0, 0, axis_index_groups=same_core, tiled=True)
    other = swapped(mine, "gz", 1)

    def big(n, rows=2 * ch):
        return pl.BlockSpec((n, rows, length_x), lambda i: (i, 0, 0))

    rows = pairs * 2 * MODES
    cells = pencils * length_x
    spectra, hidden_cot = pl.pallas_call(
        pre_kernel,
        grid=(pairs // PRE_STEP,),
        in_specs=[big(PRE_STEP), big(PRE_STEP), whole((length_x, 2 * MODES)), whole((ch, hid))],
        out_specs=[
            pl.BlockSpec((PRE_STEP, 2 * MODES, 2 * ch), lambda i: (i, 0, 0)),
            big(PRE_STEP, 2 * hid),
        ],
        out_shape=[
            jax.ShapeDtypeStruct((pairs, 2 * MODES, 2 * ch), F32),
            jax.ShapeDtypeStruct((pairs, 2 * hid, length_x), BF16),
        ],
        cost_estimate=pl.CostEstimate(
            flops=2 * cells * ch * (hid + 2 * MODES), bytes_accessed=cells * 12 * ch, transcendentals=0
        ),
        compiler_params=pltpu.CompilerParams(vmem_limit_bytes=PRE_MIB << 20),
        name="pre",
    )(u, g, analysis, down_weight.T)
    spectra = spectra.reshape(rows, 2 * ch)

    wide = kept * ch + 2 * (2 * ch // owners) + 8
    smem = pl.BlockSpec(memory_space=pltpu.SMEM)
    weights = whole((chips, kept * ch, 2 * ch))
    result, pre_grad, kept_half, sent_half, coeffs = pl.pallas_call(
        main_kernel,
        grid=(pairs // PER_STEP,),
        in_specs=[
            smem,
            whole((rows, 2 * ch)),
            weights,
            weights,
            big(PER_STEP),
            big(PER_STEP),
            big(PER_STEP, 2 * hid),
            whole((ch, ch)),
            whole((ch, hid)),
            whole((ch, hid)),
            whole((2 * MODES, length_x)),
        ],
        out_specs=[big(PER_STEP), big(PER_STEP)]
        + [whole((chips, wide, 2 * ch))] * 2
        + [whole((rows, 2 * ch))],
        out_shape=[
            jax.ShapeDtypeStruct((pairs, 2 * ch, length_x), BF16),
            jax.ShapeDtypeStruct((pairs, 2 * ch, length_x), BF16),
            jax.ShapeDtypeStruct((chips, wide, 2 * ch), F32),
            jax.ShapeDtypeStruct((chips, wide, 2 * ch), F32),
            jax.ShapeDtypeStruct((rows, 2 * ch), F32),
        ],
        scratch_shapes=[
            pltpu.VMEM((rows, 2 * ch), F32),
            pltpu.VMEM((ch, hid), F32),
            pltpu.VMEM((ch, hid), F32),
            pltpu.VMEM((2 * ch, 2 * ch), F32),
        ],
        cost_estimate=pl.CostEstimate(
            flops=16 * cells * ch * hid, bytes_accessed=cells * 16 * ch, transcendentals=cells * hid
        ),
        compiler_params=pltpu.CompilerParams(vmem_limit_bytes=MAIN_MIB << 20),
        name="main",
    )(
        core_word, spectra, mine, other, u, g, hidden_cot, skip_weight, up_weight, down_weight.T,
        synthesis.T,
    )

    chip_sum = kept_half + swapped(sent_half, "gz", 1)
    arrived = lax.all_to_all(chip_sum, "gz", 0, 0, axis_index_groups=same_core, tiled=True)

    grad_fields = pl.pallas_call(
        final_kernel,
        grid=(pairs // FINAL_STEP,),
        in_specs=[
            smem,
            whole((rows, 2 * ch)),
            weights,
            weights,
            big(FINAL_STEP),
            whole((2 * ch, 2 * ch)),
            whole((2 * MODES, length_x)),
        ],
        out_specs=big(FINAL_STEP),
        out_shape=jax.ShapeDtypeStruct((pairs, 2 * ch, length_x), BF16),
        scratch_shapes=[pltpu.VMEM((rows, 2 * ch), F32)],
        cost_estimate=pl.CostEstimate(
            flops=8 * cells * ch * ch, bytes_accessed=cells * 4 * ch, transcendentals=0
        ),
        compiler_params=pltpu.CompilerParams(vmem_limit_bytes=FINAL_MIB << 20),
        name="final",
    )(core_word, coeffs, mine, other, pre_grad, twice(skip_weight), analysis.T)

    total = jnp.sum(arrived, axis=0)
    all_pencils = pencils * rows_y * owners
    cell_scale = 1.0 / math.sqrt(length_x * all_pencils)
    pencil_scale = 1.0 / math.sqrt(all_pencils)
    at = kept * ch
    part = 2 * ch // owners
    everyone = lambda axis: [list(range(lax.axis_size(axis)))]
    small = to_group(total[at:], "gy", everyone("gy"))
    spec = total[:at]
    spec = spec + swapped(spec, "gy", 1)
    small = jnp.sum(small, axis=0) * cell_scale
    small = to_group(small, "gz", everyone("gz"))
    spec = (spec + swapped(spec, "gy", 2) + swapped(spec, "gy", 4) + swapped(spec, "gy", 6)) * pencil_scale
    grad_spec = spec.reshape(kept, ch, 2, ch).transpose(0, 2, 1, 3)

    def joined(block):
        return block.reshape(2, ch, 2 * ch).transpose(1, 0, 2).reshape(ch, hid)

    grad_up = joined(small[:, :part])
    grad_down = joined(small[:, part : 2 * part]).T
    grad_skip = small[:, 2 * part : 2 * part + ch // owners, :ch].reshape(ch, ch)

    def unpacked(x):
        return x.reshape(count_y, count_z, ch, length_x).transpose(3, 0, 1, 2)

    return (unpacked(result), unpacked(grad_fields), grad_spec, grad_skip, grad_up, grad_down)


def solution(mesh):
    big = P(None, "gy", "gz", None)
    modes = P("gz", None, None, None)

    return jax.shard_map(
        local,
        mesh=mesh,
        in_specs=(big, modes, P(), P(), P(), big),
        out_specs=(big, big, modes, P(), P(), P()),
        check_vma=False,
    )
```

```python
import math

import jax
import jax.numpy as jnp
import numpy as np
from jax import lax
from jax.experimental import pallas as pl
from jax.experimental.pallas import tpu as pltpu
from jax.sharding import PartitionSpec as P

MODES = 32
BF16 = jnp.bfloat16
F32 = jnp.float32
CHUNK = 256
PER_STEP = 2
FINAL_STEP = 4
PRE_STEP = 4
PRE_CHUNK = 1024
SKEW = 2
UNROLL = 4
PRE_MIB = 60
MAIN_MIB = 50
FINAL_MIB = 50


def to_group(block, axis, groups):
    peers = len(groups[0])
    return lax.all_to_all(
        jnp.broadcast_to(block[None], (peers, *block.shape)),
        axis, 0, 0, axis_index_groups=groups, tiled=True,
    )


def swapped(block, axis, mask):
    return lax.ppermute(block, axis, [(i, i ^ mask) for i in range(lax.axis_size(axis))])


def fourier_tables(length_x, kept):
    phase = np.outer(np.arange(length_x), np.arange(kept)) % length_x * (2.0 * np.pi / length_x)
    table = np.concatenate([np.cos(phase), -np.sin(phase)], axis=1) / math.sqrt(length_x)
    doubled = np.where(np.arange(2 * kept) % kept == 0, 1.0, 2.0)
    return table.astype(BF16), (table * doubled).astype(BF16)


def mm(a, b):
    return jnp.dot(a, b, preferred_element_type=F32)


def mm_nt(a, b):
    return lax.dot_general(a, b, (((1,), (1,)), ((), ())), preferred_element_type=F32)


def mm_tn(a, b):
    return lax.dot_general(a, b, (((0,), (0,)), ((), ())), preferred_element_type=F32)


def high_low(x):
    high = x.astype(BF16)
    return high, (x - high.astype(F32)).astype(BF16)


def gelu_pair(y):
    c = math.sqrt(2.0 / math.pi)
    a = 0.044715
    k = lambda v: jnp.asarray(v, y.dtype)
    y2 = y * y
    t = jnp.tanh(y * (y2 * k(8.0 * c * a) + k(2.0 * c)))
    top = t + k(1.0)
    g = y * top
    slope = top + (g - g * t) * (y2 * k(24.0 * c * a) + k(2.0 * c))
    return g, slope


def split_lanes(even, odd):
    half = even.shape[-1] // 2
    first = lax.broadcasted_iota(jnp.int32, even.shape, 1) < half
    low = jnp.where(first, even, pltpu.roll(odd, half, 1))
    high = jnp.where(first, pltpu.roll(even, half, 1), odd)
    return low, high


def mode_rows(ref, k, pairs):
    stride = 2 * MODES
    re = ref[pl.ds(k, pairs, stride=stride), :]
    im = ref[pl.ds(MODES + k, pairs, stride=stride), :]
    return jnp.concatenate(split_lanes(re, im), axis=0)


def put_mode_rows(ref, k, pairs, rows):
    stride = 2 * MODES
    re, im = split_lanes(rows[:pairs], rows[pairs:])
    ref[pl.ds(k, pairs, stride=stride), :] = re
    ref[pl.ds(MODES + k, pairs, stride=stride), :] = im


def mixer_of(upper):
    half = upper.shape[-1] // 2
    sign = jnp.where(lax.broadcasted_iota(jnp.int32, upper.shape, 1) < half, -1.0, 1.0)
    return jnp.concatenate([upper, pltpu.roll(upper, half, 1) * sign], axis=0)


def each_mode(core, mine_ref, other_ref, ch, visit):
    kept = mine_ref.shape[1] // ch

    @pl.loop(0, mine_ref.shape[0], unroll=UNROLL)
    def _(chip):
        for side, ref in enumerate((mine_ref, other_ref)):
            for i in range(kept):
                visit((chip * 2 + (core ^ side)) * kept + i, ref[chip, i * ch : (i + 1) * ch, :])


def copies_kernel(w_ref, out_ref):
    kept, _, ch, _ = w_ref.shape
    for i in range(kept):
        upper = jnp.concatenate([w_ref[i, 0], w_ref[i, 1]], axis=1)
        for chip in range(out_ref.shape[0]):
            out_ref[chip, i * ch : (i + 1) * ch, :] = upper


def pre_kernel(u_ref, g_ref, ana_ref, down_t_ref, t_ref, hc_ref):
    ch, hid = down_t_ref.shape
    length_x = u_ref.shape[-1]
    down = down_t_ref[...].T * BF16(0.5)
    for i in range(u_ref.shape[0]):
        t_ref[i] = mm(u_ref[i], ana_ref[...]).T
        for j in range(length_x // PRE_CHUNK):
            span = slice(j * PRE_CHUNK, (j + 1) * PRE_CHUNK)
            for b in range(2):
                hc = mm(down, g_ref[i, b * ch : (b + 1) * ch, span])
                hc_ref[i, b * hid : (b + 1) * hid, span] = hc.astype(BF16)


def main_kernel(
    core_ref, t_ref, mine_ref, other_ref, u_ref, g_ref, hc_ref, skip_ref, up_ref, down_t_ref,
    syn_ref,
    res_ref, pg_ref, kept_ref, sent_ref, c_ref,
    m_ref, gu_ref, gd_ref, gs_ref,
):
    q = pl.program_id(0)
    steps = pl.num_programs(0)
    n_pairs = t_ref.shape[0] // (2 * MODES)
    per_step = u_ref.shape[0]
    length_x = u_ref.shape[-1]
    ch, hid = up_ref.shape

    @pl.when(q == 0)
    def _():
        gu_ref[...] = jnp.zeros_like(gu_ref)
        gd_ref[...] = jnp.zeros_like(gd_ref)
        gs_ref[...] = jnp.zeros_like(gs_ref)

        def visit(k, upper):
            rows, rows_low = high_low(mode_rows(t_ref, k, n_pairs))
            mixer, mixer_low = high_low(mixer_of(upper))
            mixed = mm(
                jnp.concatenate([rows, rows_low], axis=1), jnp.concatenate([mixer, mixer], axis=0)
            )
            put_mode_rows(m_ref, k, n_pairs, mixed + mm(rows, mixer_low))

        each_mode(core_ref[0], mine_ref, other_ref, ch, visit)

    up = up_ref[...] * BF16(0.5)
    up_t, down_t = up.T, down_t_ref[...]
    skip_t = (twice(skip_ref[...].astype(F32).T) * 0.5).astype(BF16)
    chunks = length_x // CHUNK
    n = per_step * chunks * 2
    span = lambda j: slice(j % chunks * CHUNK, (j % chunks + 1) * CHUNK)
    lane = lambda b: slice(b * ch, (b + 1) * ch)
    unit = lambda b: slice(b * hid, (b + 1) * hid)
    lhs_pre, pre, acts, hps, hids, outs, grads, accs = {}, {}, {}, {}, {}, {}, {}, {}
    total = {}

    def add(where, key, value):
        where[key] = where[key] + value if key in where else value

    def base(p):
        return pl.multiple_of((q * per_step + p) * (2 * MODES), 2 * MODES)

    def table_rows(j):
        return jnp.concatenate([u_ref[j // chunks, :, span(j)], syn_ref[:, span(j)]], axis=0)

    def first(j):
        p = j // chunks
        if j % chunks == 0:
            mixed, mixed_low = high_low(m_ref[pl.ds(base(p), 2 * MODES), :].T * 0.5)
            lhs_pre[p] = jnp.concatenate([skip_t, mixed, mixed_low], axis=1)
        rhs = jnp.concatenate([table_rows(j), syn_ref[:, span(j)]], axis=0)
        pre[j] = mm(lhs_pre[p], rhs)

    def gelu_act(j):
        act, slope = gelu_pair(pre.pop(j))
        acts[j] = (act.astype(BF16), slope)

    def widen(i):
        j, b = divmod(i, 2)
        hps[i] = mm(up_t, acts[j][0][lane(b)]).astype(BF16)

    def gelu_hidden(i):
        j, b = divmod(i, 2)
        hidden, slope = gelu_pair(hps.pop(i))
        hids[i] = (hidden, hc_ref[j // chunks, unit(b), span(j)] * slope)

    def narrow(i):
        j, b = divmod(i, 2)
        hidden, hgrad = hids.pop(i)
        outs[i] = mm(down_t, hidden)
        grads[i] = mm(up, hgrad)
        add(total, "gd", mm_nt(g_ref[j // chunks, lane(b), span(j)], hidden))
        add(total, "gu", mm_nt(acts[j][0][lane(b)], hgrad))

    def last(j):
        p = j // chunks
        out = jnp.concatenate([outs.pop(2 * j), outs.pop(2 * j + 1)], axis=0)
        res_ref[p, :, span(j)] = out.astype(BF16)
        both = jnp.concatenate([grads.pop(2 * j), grads.pop(2 * j + 1)], axis=0)
        pg = (both * acts.pop(j)[1]).astype(BF16)
        pg_ref[p, :, span(j)] = pg
        add(accs, p, mm_nt(table_rows(j), pg))
        if j % chunks == chunks - 1:
            acc = accs.pop(p)
            add(total, "gs", acc[: 2 * ch])
            c_ref[pl.ds(base(p), 2 * MODES), :] = acc[2 * ch :]

    ahead = SKEW * 2
    for i in range(-ahead, n + 2):
        j, b = divmod(i + ahead, 2)
        if b == 0 and 0 <= j < n // 2:
            first(j)
            gelu_act(j)
        if 0 <= i + 1 < n:
            widen(i + 1)
        if 0 <= i < n:
            gelu_hidden(i)
        if 0 <= i - 1 < n:
            narrow(i - 1)
            if (i - 1) % 2 == 1:
                last((i - 1) // 2)
    gu_ref[...] += total["gu"]
    gd_ref[...] += total["gd"]
    gs_ref[...] += total["gs"]

    @pl.when(q == steps - 1)
    def _():
        chips = kept_ref.shape[0]
        kept = MODES // (2 * chips)
        mine = core_ref[0]
        sign = jnp.where(lax.broadcasted_iota(jnp.int32, (ch, 2 * ch), 1) < ch, 1.0, -1.0)

        @pl.loop(0, chips, unroll=UNROLL)
        def _(chip):
            for side, ref in enumerate((kept_ref, sent_ref)):
                for i in range(kept):
                    k = (chip * 2 + (mine ^ side)) * kept + i
                    spec = mode_rows(t_ref, k, n_pairs).astype(BF16)
                    coef = mode_rows(c_ref, k, n_pairs).astype(BF16)
                    moment = mm_tn(spec, coef)
                    grad = moment[:ch] + pltpu.roll(moment[ch:], ch, 1) * sign
                    ref[chip, i * ch : (i + 1) * ch, :] = grad

        at = kept * ch
        part = ch // chips
        gs_ref[:ch] += pltpu.roll(gs_ref[ch:], ch, 1)
        small = ch // (2 * chips)
        for chip in range(chips):
            half_at = slice(chip // (chips // 2) * 2 * ch, (chip // (chips // 2) + 1) * 2 * ch)
            for side, ref in enumerate((kept_ref, sent_ref)):
                o = chip * 2 + (mine ^ side)
                rows = pl.ds(pl.multiple_of(o % chips * part, part), part)
                ref[chip, at : at + part, :] = gu_ref[rows, half_at]
                ref[chip, at + part : at + 2 * part, :] = gd_ref[rows, half_at]
                ref[chip, at + 2 * part : at + 2 * part + 8, :] = jnp.zeros((8, 2 * ch), F32)
                ref[chip, at + 2 * part : at + 2 * part + small, :] = gs_ref[pl.ds(o * small, small), :]


def final_kernel(core_ref, c_ref, mine_ref, other_ref, pg_ref, skip_ref, ana_ref, out_ref, b_ref):
    q = pl.program_id(0)
    n_pairs = c_ref.shape[0] // (2 * MODES)
    per_step = pg_ref.shape[0]

    @pl.when(q == 0)
    def _():
        def visit(k, upper):
            coef = mode_rows(c_ref, k, n_pairs).astype(BF16)
            put_mode_rows(b_ref, k, n_pairs, mm_nt(coef, mixer_of(upper).astype(BF16)))

        each_mode(core_ref[0], mine_ref, other_ref, skip_ref.shape[0] // 2, visit)

    for p in range(per_step):
        base = pl.multiple_of((q * per_step + p) * (2 * MODES), 2 * MODES)
        back, back_low = high_low(b_ref[pl.ds(base, 2 * MODES), :].T)
        lhs = jnp.concatenate([skip_ref[...], back, back_low], axis=1)
        rhs = jnp.concatenate([pg_ref[p], ana_ref[...], ana_ref[...]], axis=0)
        out_ref[p] = mm(lhs, rhs).astype(BF16)


def unpack_kernel(scale, a_ref, b_ref, c_ref, d_ref, small_ref, spec_ref, skip_ref, up_ref, down_ref):
    spec = (a_ref[...] + b_ref[...] + c_ref[...] + d_ref[...]) * scale
    kept, _, ch, _ = spec_ref.shape
    for i in range(kept):
        for r in range(2):
            spec_ref[i, r] = spec[i * ch : (i + 1) * ch, r * ch : (r + 1) * ch]
    owners = small_ref.shape[0]
    part = 2 * ch // owners
    rows = ch // owners
    for o in range(owners):
        side, row = divmod(o, owners // 2)
        at = slice(row * part, (row + 1) * part)
        lanes = slice(side * 2 * ch, (side + 1) * 2 * ch)
        up_ref[at, lanes] = small_ref[o, :part]
        down_ref[at, lanes] = small_ref[o, part : 2 * part]
        skip_ref[o * rows : (o + 1) * rows] = small_ref[o, 2 * part : 2 * part + rows, :ch]


def twice(weight):
    zeros = jnp.zeros_like(weight)
    upper = jnp.concatenate([weight, zeros], axis=1)
    lower = jnp.concatenate([zeros, weight], axis=1)
    return jnp.concatenate([upper, lower], axis=0)


def whole(shape):
    return pl.BlockSpec(shape, lambda *_: (0,) * len(shape))


def local(fields, spec_weight, skip_weight, up_weight, down_weight, cotangent):
    length_x, count_y, count_z, ch = fields.shape
    hid = up_weight.shape[1]
    pencils = count_y * count_z
    pairs = pencils // 2
    owners = lax.axis_size("gz")
    rows_y = lax.axis_size("gy")
    chips = owners // 2
    kept = MODES // owners
    analysis, synthesis = fourier_tables(length_x, MODES)
    u = fields.transpose(1, 2, 3, 0).reshape(pairs, 2 * ch, length_x)
    g = cotangent.transpose(1, 2, 3, 0).reshape(pairs, 2 * ch, length_x)
    core = lax.axis_index("gz") % 2
    core_word = jnp.full((1,), core, jnp.int32)
    same_core = [[i for i in range(owners) if i % 2 == c] for c in range(2)]

    copies = pl.pallas_call(
        copies_kernel,
        out_shape=jax.ShapeDtypeStruct((chips, kept * ch, 2 * ch), F32),
        name="copies",
    )(spec_weight)
    mine = lax.all_to_all(copies, "gz", 0, 0, axis_index_groups=same_core, tiled=True)
    other = swapped(mine, "gz", 1)

    def big(n, rows=2 * ch):
        return pl.BlockSpec((n, rows, length_x), lambda i: (i, 0, 0))

    rows = pairs * 2 * MODES
    cells = pencils * length_x
    spectra, hidden_cot = pl.pallas_call(
        pre_kernel,
        grid=(pairs // PRE_STEP,),
        in_specs=[big(PRE_STEP), big(PRE_STEP), whole((length_x, 2 * MODES)), whole((ch, hid))],
        out_specs=[
            pl.BlockSpec((PRE_STEP, 2 * MODES, 2 * ch), lambda i: (i, 0, 0)),
            big(PRE_STEP, 2 * hid),
        ],
        out_shape=[
            jax.ShapeDtypeStruct((pairs, 2 * MODES, 2 * ch), F32),
            jax.ShapeDtypeStruct((pairs, 2 * hid, length_x), BF16),
        ],
        cost_estimate=pl.CostEstimate(
            flops=2 * cells * ch * (hid + 2 * MODES), bytes_accessed=cells * 12 * ch, transcendentals=0
        ),
        compiler_params=pltpu.CompilerParams(vmem_limit_bytes=PRE_MIB << 20),
        name="pre",
    )(u, g, analysis, down_weight.T)
    spectra = spectra.reshape(rows, 2 * ch)

    wide = kept * ch + 2 * (2 * ch // owners) + 8
    smem = pl.BlockSpec(memory_space=pltpu.SMEM)
    weights = whole((chips, kept * ch, 2 * ch))
    result, pre_grad, kept_half, sent_half, coeffs = pl.pallas_call(
        main_kernel,
        grid=(pairs // PER_STEP,),
        in_specs=[
            smem,
            whole((rows, 2 * ch)),
            weights,
            weights,
            big(PER_STEP),
            big(PER_STEP),
            big(PER_STEP, 2 * hid),
            whole((ch, ch)),
            whole((ch, hid)),
            whole((ch, hid)),
            whole((2 * MODES, length_x)),
        ],
        out_specs=[big(PER_STEP), big(PER_STEP)]
        + [whole((chips, wide, 2 * ch))] * 2
        + [whole((rows, 2 * ch))],
        out_shape=[
            jax.ShapeDtypeStruct((pairs, 2 * ch, length_x), BF16),
            jax.ShapeDtypeStruct((pairs, 2 * ch, length_x), BF16),
            jax.ShapeDtypeStruct((chips, wide, 2 * ch), F32),
            jax.ShapeDtypeStruct((chips, wide, 2 * ch), F32),
            jax.ShapeDtypeStruct((rows, 2 * ch), F32),
        ],
        scratch_shapes=[
            pltpu.VMEM((rows, 2 * ch), F32),
            pltpu.VMEM((ch, hid), F32),
            pltpu.VMEM((ch, hid), F32),
            pltpu.VMEM((2 * ch, 2 * ch), F32),
        ],
        cost_estimate=pl.CostEstimate(
            flops=16 * cells * ch * hid, bytes_accessed=cells * 16 * ch, transcendentals=cells * hid
        ),
        compiler_params=pltpu.CompilerParams(vmem_limit_bytes=MAIN_MIB << 20),
        name="main",
    )(
        core_word, spectra, mine, other, u, g, hidden_cot, skip_weight, up_weight, down_weight.T,
        synthesis.T,
    )

    chip_sum = kept_half + swapped(sent_half, "gz", 1)
    arrived = lax.all_to_all(chip_sum, "gz", 0, 0, axis_index_groups=same_core, tiled=True)

    grad_fields = pl.pallas_call(
        final_kernel,
        grid=(pairs // FINAL_STEP,),
        in_specs=[
            smem,
            whole((rows, 2 * ch)),
            weights,
            weights,
            big(FINAL_STEP),
            whole((2 * ch, 2 * ch)),
            whole((2 * MODES, length_x)),
        ],
        out_specs=big(FINAL_STEP),
        out_shape=jax.ShapeDtypeStruct((pairs, 2 * ch, length_x), BF16),
        scratch_shapes=[pltpu.VMEM((rows, 2 * ch), F32)],
        cost_estimate=pl.CostEstimate(
            flops=8 * cells * ch * ch, bytes_accessed=cells * 4 * ch, transcendentals=0
        ),
        compiler_params=pltpu.CompilerParams(vmem_limit_bytes=FINAL_MIB << 20),
        name="final",
    )(core_word, coeffs, mine, other, pre_grad, twice(skip_weight), analysis.T)

    total = jnp.sum(arrived, axis=0)
    all_pencils = pencils * rows_y * owners
    cell_scale = 1.0 / math.sqrt(length_x * all_pencils)
    pencil_scale = 1.0 / math.sqrt(all_pencils)
    at = kept * ch
    everyone = lambda axis: [list(range(lax.axis_size(axis)))]
    small = to_group(total[at:], "gy", everyone("gy"))
    spec = total[:at]
    spec = spec + swapped(spec, "gy", 1)
    small = jnp.sum(small, axis=0) * cell_scale
    small = to_group(small, "gz", everyone("gz"))
    parts = [spec] + [swapped(spec, "gy", mask) for mask in (2, 4, 6)]
    grad_spec, grad_skip, grad_up, down_t = pl.pallas_call(
        lambda *refs: unpack_kernel(pencil_scale, *refs),
        out_shape=[
            jax.ShapeDtypeStruct((kept, 2, ch, ch), F32),
            jax.ShapeDtypeStruct((ch, ch), F32),
            jax.ShapeDtypeStruct((ch, hid), F32),
            jax.ShapeDtypeStruct((ch, hid), F32),
        ],
        compiler_params=pltpu.CompilerParams(vmem_limit_bytes=8 << 20),
        name="unpack",
    )(*parts, small)
    grad_down = down_t.T

    def unpacked(x):
        return x.reshape(count_y, count_z, ch, length_x).transpose(3, 0, 1, 2)

    return (unpacked(result), unpacked(grad_fields), grad_spec, grad_skip, grad_up, grad_down)


def solution(mesh):
    big = P(None, "gy", "gz", None)
    modes = P("gz", None, None, None)

    return jax.shard_map(
        local,
        mesh=mesh,
        in_specs=(big, modes, P(), P(), P(), big),
        out_specs=(big, big, modes, P(), P(), P()),
        check_vma=False,
    )
```
